256 devices in a mesh: lat: 16 (over z, core), lon: 16 (over y, x).
Axes of the slice: x: 4, y: 4, z: 8, core: 2. Of those that a mesh axis runs over, the one named last changes fastest.
Arguments:
- density: float32 [75, 256, 4096], P(None, 'lat', 'lon'), may hold values from -24 to 24
- tend_east: float32 [75, 256, 4096], P(None, 'lat', 'lon'), may hold values from -6 to 6
- tend_north: float32 [75, 256, 4096], P(None, 'lat', 'lon'), may hold values from -6 to 6
- thickness: float32 [75], replicated, may hold values from 0.02 to 0.2
- levels: int32 [256, 4096], P('lat', 'lon'), may hold values from 1 to 75
- ocean_mask: int32 [256, 4096], P('lat', 'lon'), may hold values 0 or 1
- eta_prev: float32 [256, 4096], P('lat', 'lon'), may hold values from -1.2 to 1.2
- coarse: float32 [4096, 4096], P(('lat', 'lon')), as said below
Outputs:
- surface: float32 [256, 4096], P('lat', 'lon')
- precond_residual: float32 [256, 4096], P('lat', 'lon')
The draws below stay inside these ranges and needn't reach their ends.
Inputs may be any that keep to these rules, and one draw needn't show every extreme that they name: coarse is symmetric positive definite.
All inputs are finite; a program needn't handle non-finite values. No bound on the sum of `ocean_mask` on one device may be relied on, other than what follows from the above.
Results may differ from the reference program's by a relative error of at most 0.0003.
Values sent between devices are 32-bit elements; how exact they have to be, the bound alone decides.
No kernel may reach another device: no remote copies, remote signals or barrier semaphores. Data moves between devices by JAX's collectives and lax.ppermute only.
A program may use at most 64 MiB of HBM per device.

```python
import math
import jax
import jax.numpy as jnp
from jax import lax

K = 75
TILE_SIDE = 4
ITERS = 2
CA = 16
CL = 256
NA = 256
NL = 4096
COARSE = 4096
N_LAT = 16
N_LON = 16


def draw_levels(key, part):
    row_index = lax.broadcasted_iota(jnp.int32, (NA, NL), 0)
    col_index = lax.broadcasted_iota(jnp.int32, (NA, NL), 1)
    shallow = K // 4
    ceiling = shallow + (K - shallow) * row_index // max(NA - 1, 1)
    drawn_bits = jax.random.randint(key, (NA, NL), 0, 1 << 20)
    level_counts = 1 + drawn_bits % ceiling
    corner = jnp.logical_and(row_index == NA - 1, col_index == 0)
    return jnp.where(corner, K, level_counts).astype(jnp.int32)


def draw_coarse(key, part):
    scale_key = jax.random.fold_in(key, 11)
    noise_key = jax.random.fold_in(key, 23)
    scales = jnp.exp(jax.random.uniform(scale_key, (COARSE,), jnp.float32, jnp.log(0.002), jnp.log(0.02)))
    noise_draw = jax.random.normal(noise_key, (COARSE, COARSE), jnp.float32)
    symmetric = (noise_draw + noise_draw.T) * (0.4 / jnp.sqrt(2.0 * COARSE))
    root_scale = jnp.sqrt(scales)
    matrix = root_scale[:, None] * (jnp.eye(COARSE, dtype=jnp.float32) + symmetric) * root_scale[None, :]
    return matrix.astype(jnp.float32)


def place_ends(entries, own_key, low, high):
    extent = entries.shape
    spot = [jax.random.randint(jax.random.fold_in(own_key, axis), (), 0, extent[axis]) for axis in range(len(extent))]
    entries = entries.at[tuple(spot)].set(low)
    longest = extent.index(max(extent))
    spot[longest] = (spot[longest] + 1) % extent[longest]
    return entries.at[tuple(spot)].set(high)


def steps_of(own_key, extent, split, smallest, top_value):
    gain = 1.0
    for position, shards_of in split:
        heights = jax.random.uniform(jax.random.fold_in(jax.random.fold_in(own_key, 6), position), (shards_of,), jnp.float32, smallest / len(split), top_value / len(split))
        gain = gain * jnp.repeat(jnp.exp(heights), extent[position] // shards_of).reshape((-1,) + (1,) * (len(extent) - 1 - position))
    return gain


def centred(stream_key, extent, deviation, reach, shards=(), held_as=jnp.bfloat16):
    result = deviation * jax.random.normal(stream_key, extent, jnp.float32)
    if shards:
        result = result * steps_of(stream_key, extent, shards, -0.22, 0.18)
    return jnp.clip(result, -reach, reach).astype(held_as)


def setup_inputs(seed: int = 0) -> dict:
    streams_of = jax.random.split(jax.random.key(seed), 9)
    return {
        "density": centred(streams_of[0], (K, NA, NL), 4.0, 24.0, ((1, 16), (2, 16)), jnp.float32),
        "tend_east": centred(streams_of[1], (K, NA, NL), 1.0, 6.0, ((1, 16), (2, 16)), jnp.float32),
        "tend_north": centred(streams_of[2], (K, NA, NL), 1.0, 6.0, ((1, 16), (2, 16)), jnp.float32),
        "thickness": jnp.clip(jnp.exp(jax.random.uniform(streams_of[3], (K,), jnp.float32, math.log(0.02), math.log(0.2))), 0.02, 0.2),
        "levels": draw_levels(jax.random.fold_in(streams_of[8], 71), 0),
        "ocean_mask": place_ends((jax.random.randint(streams_of[5], (NA, NL), 0, 10) < 7).astype(jnp.int32), jax.random.fold_in(streams_of[5], 1), 0, 1),
        "eta_prev": centred(streams_of[6], (NA, NL), 0.2, 1.2, ((0, 16), (1, 16)), jnp.float32),
        "coarse": draw_coarse(jax.random.fold_in(streams_of[8], 71), 0),
    }


surface_coeff = 0.25
highest = lax.Precision.HIGHEST


def padded_grid(values, rim_width):
    leading = [(0, 0)] * (values.ndim - 2)
    framed = jnp.pad(values, leading + [(rim_width, rim_width), (0, 0)])
    return jnp.concatenate([framed[..., -rim_width:], framed, framed[..., :rim_width]], axis=-1)


def restrict(values, ocean_share):
    tiled_sum = (values * ocean_share).reshape(N_LAT, TILE_SIDE, CA // TILE_SIDE, N_LON, TILE_SIDE, CL // TILE_SIDE)
    return jnp.sum(tiled_sum, axis=(2, 5)).transpose(0, 2, 1, 3).reshape(-1)


def prolong(coarse_values, ocean_share):
    blocks = coarse_values.reshape(N_LAT, N_LON, TILE_SIDE, TILE_SIDE).transpose(0, 2, 1, 3)
    spread = jnp.broadcast_to(blocks[:, :, None, :, :, None], (N_LAT, TILE_SIDE, CA // TILE_SIDE, N_LON, TILE_SIDE, CL // TILE_SIDE))
    return spread.reshape(NA, NL) * ocean_share


def reference(density, tend_east, tend_north, thickness, levels, ocean_mask, eta_prev, coarse):
    wet_levels = levels * ocean_mask
    ocean_share = ocean_mask.astype(jnp.float32)
    level_index = jnp.arange(K, dtype=jnp.int32)

    def level_step(carry, level_inputs):
        running, column_depth, force_east, force_north = carry
        layer_density, layer_east, layer_north, layer_thickness, level = level_inputs
        running = running + layer_thickness * layer_density
        layer_active = (level < wet_levels).astype(jnp.float32)
        layer_pressure = running * layer_active
        framed = padded_grid(layer_pressure, 2)
        own_rows = framed[2:-2, :]
        east_diff = (8.0 * (own_rows[:, 3:-1] - own_rows[:, 1:-3]) - (own_rows[:, 4:] - own_rows[:, :-4])) / 12.0
        own_cols = framed[:, 2:-2]
        north_diff = (8.0 * (own_cols[3:-1, :] - own_cols[1:-3, :]) - (own_cols[4:, :] - own_cols[:-4, :])) / 12.0
        column_depth = column_depth + layer_thickness * layer_active
        force_east = force_east + layer_thickness * layer_active * (layer_east - east_diff)
        force_north = force_north + layer_thickness * layer_active * (layer_north - north_diff)
        return (running, column_depth, force_east, force_north), None

    zero_plane = jnp.zeros((NA, NL), jnp.float32)
    carried, _ = lax.scan(level_step, (zero_plane, zero_plane, zero_plane, zero_plane), (density, tend_east, tend_north, thickness, level_index))
    column_depth = carried[1]
    forcing = padded_grid(jnp.stack([carried[2], carried[3]]), 1)
    right_side = ocean_share * 0.5 * (forcing[0, 1:-1, :-2] - forcing[0, 1:-1, 2:] + forcing[1, :-2, 1:-1] - forcing[1, 2:, 1:-1])
    depth_framed = padded_grid(column_depth, 1)
    center = depth_framed[1:-1, 1:-1]
    east_face = jnp.minimum(center, depth_framed[1:-1, 2:])
    west_face = jnp.minimum(center, depth_framed[1:-1, :-2])
    north_face = jnp.minimum(center, depth_framed[2:, 1:-1])
    south_face = jnp.minimum(center, depth_framed[:-2, 1:-1])
    diagonal = ocean_share * (surface_coeff + east_face + west_face + north_face + south_face) + (1.0 - ocean_share)

    def operate(values):
        beside_all = padded_grid(values, 1)
        return diagonal * values - (east_face * beside_all[1:-1, 2:] + west_face * beside_all[1:-1, :-2] + north_face * beside_all[2:, 1:-1] + south_face * beside_all[:-2, 1:-1])

    def precondition(values):
        return values / diagonal + prolong(jnp.dot(coarse, restrict(values, ocean_share), precision=highest), ocean_share)

    solution = ocean_share * eta_prev
    residual = right_side - operate(solution)
    precond = precondition(residual)
    direction = precond
    rz_now = jnp.sum(residual * precond)
    for iteration in range(ITERS):
        image_field = operate(direction)
        step_length = rz_now / jnp.sum(direction * image_field)
        solution = solution + step_length * direction
        residual = residual - step_length * image_field
        precond = precondition(residual)
        rz_next = jnp.sum(residual * precond)
        direction = precond + (rz_next / rz_now) * direction
        rz_now = rz_next
    return solution, precond
```

```python
import jax
import jax.numpy as jnp
from jax import lax
from jax.experimental import pallas as pl
from jax.experimental.pallas import tpu as pltpu
from jax.sharding import PartitionSpec as P

K = 75
KB = 15
R = 16
L = 256
H = 128
NLON = 16
NLAT = 16
NDEV = 256
EPS = 0.25
f32 = jnp.float32
highest = lax.Precision.HIGHEST
BOTH = ("lat", "lon")


def iota(shape, dim):
    return lax.broadcasted_iota(jnp.int32, shape, dim)


def call(kernel, out_shapes, name, **kw):
    vm = pl.BlockSpec(memory_space=pltpu.VMEM)
    n_out = len(out_shapes)

    def run(*args):
        return pl.pallas_call(
            kernel,
            out_shape=[jax.ShapeDtypeStruct(s, f32) for s in out_shapes],
            in_specs=[vm] * len(args),
            out_specs=[vm] * n_out,
            name=name,
            **kw,
        )(*args)

    return run


def east(v, edge):
    return jnp.where(iota((R, L), 1) == L - 1, edge, pltpu.roll(v, L - 1, 1))


def west(v, edge):
    return jnp.where(iota((R, L), 1) == 0, edge, pltpu.roll(v, 1, 1))


def north(v, edge):
    return jnp.where(iota((R, L), 0) == R - 1, edge, pltpu.roll(v, R - 1, 0))


def south(v, edge):
    return jnp.where(iota((R, L), 0) == 0, edge, pltpu.roll(v, 1, 0))


def tile_sums(fields):
    n = len(fields)
    pick = (iota((L, H), 0) // 64 == iota((L, H), 1) % 4).astype(f32)
    cols = jnp.dot(jnp.concatenate(fields, axis=0), pick, precision=highest, preferred_element_type=f32)
    keep = iota((R, H), 0) // 4 == (iota((R, H), 1) % 16) // 4
    return [
        jnp.sum(jnp.where(keep, cols[R * i : R * i + R], 0.0), axis=0, keepdims=True)
        for i in range(n)
    ]


def pack(rows, rho):
    block = iota((1, H), 1) // 16
    out = jnp.zeros((1, H), f32)
    for f, row in enumerate(rows):
        out = jnp.where(block == (f + rho) % 8, row, out)
    return jnp.broadcast_to(out, (NDEV, H))


def unpack(got, f):
    shape = (NDEV // 8, 8, H)
    keep = iota(shape, 2) // 16 == (iota(shape, 1) + f) % 8
    flat = jnp.sum(jnp.where(keep, got.reshape(shape), 0.0), axis=1)
    return pltpu.roll(flat, (H - 16 * f) % H, 1) if f else flat


def coarse_rows(c_ref, w):
    acc = jnp.zeros((R, H), f32)
    for r in range(NDEV // 8):
        acc = acc + c_ref[:, H * r : H * r + H] * w[r : r + 1, :]
    col = jnp.sum(acc, axis=1, keepdims=True)
    return jnp.sum(jnp.where(iota((R, H), 0) == iota((R, H), 1) % 16, col, 0.0), axis=0, keepdims=True)


G = (NDEV // 8, H)


def c_east(q):
    lane = iota(G, 1)
    near = pltpu.roll(q, H - 1, 1)
    far = pltpu.roll(q, H - 13, 1)
    swap = jnp.where(iota(G, 0) % 2 == 0, pltpu.roll(far, G[0] - 1, 0), pltpu.roll(far, 1, 0))
    far = jnp.where(lane // 16 == 7, swap, far)
    return jnp.where(lane % 4 == 3, far, near)


def c_west(q):
    lane = iota(G, 1)
    near = pltpu.roll(q, 1, 1)
    far = pltpu.roll(q, 13, 1)
    swap = jnp.where(iota(G, 0) % 2 == 0, pltpu.roll(far, G[0] - 1, 0), pltpu.roll(far, 1, 0))
    far = jnp.where(lane // 16 == 0, swap, far)
    return jnp.where(lane % 4 == 0, far, near)


def c_north(q):
    near = pltpu.roll(q, H - 4, 1)
    far = pltpu.roll(pltpu.roll(q, 12, 1), G[0] - 2, 0)
    return jnp.where((iota(G, 1) % 16) // 4 == 3, far, near)


def c_south(q):
    near = pltpu.roll(q, 4, 1)
    far = pltpu.roll(pltpu.roll(q, H - 12, 1), 2, 0)
    return jnp.where((iota(G, 1) % 16) // 4 == 0, far, near)


def coarse_operator(q, count, link_e, link_n):
    flux_e = link_e * (q - c_east(q))
    flux_n = link_n * (q - c_north(q))
    return EPS * count * q + (flux_e - c_west(flux_e)) + (flux_n - c_south(flux_n))


def total(v):
    return jnp.sum(jnp.sum(v, axis=0, keepdims=True), axis=1, keepdims=True)


def spread(got_ref, la, lo):
    lane = iota((1, H), 1)

    def row_of(a, o):
        return got_ref[pl.ds(a * NLON + o, 1), :]

    e_lo = (lo + 1) % NLON
    w_lo = (lo + NLON - 1) % NLON
    n_la = jnp.minimum(la + 1, NLAT - 1)
    s_la = jnp.maximum(la - 1, 0)
    row = iota((24, H), 0)
    lane24 = iota((24, H), 1)
    mine = jnp.broadcast_to(row_of(la, lo), (24, H))
    up = jnp.broadcast_to(row_of(n_la, lo), (24, H))
    down = jnp.broadcast_to(row_of(s_la, lo), (24, H))
    src = jnp.where(row < R, mine, jnp.where(row == R, up, down))
    want = jnp.where(row < R, row // 4, jnp.where(row == R, 0, 3))
    keep = (lane24 // 16 == lo % 8) & ((lane24 % 16) // 4 == want)
    pick = (iota((H, L), 0) % 4 == iota((H, L), 1) // 64).astype(f32)
    field = jnp.dot(jnp.where(keep, src, 0.0), pick, precision=highest, preferred_element_type=f32)

    def side(o, tx):
        got = jnp.broadcast_to(row_of(la, o), (R, H))
        hit = (iota((R, H), 1) // 16 == o % 8) & (iota((R, H), 1) % 16 == (iota((R, H), 0) // 4) * 4 + tx)
        return jnp.sum(jnp.where(hit, got, 0.0), axis=1, keepdims=True)

    return field[:R], side(e_lo, 0), side(w_lo, 3), field[R : R + 1], field[R + 1 : R + 2]


def prolong_row(q_row):
    keep = (iota((R, H), 1) < 16) & (iota((R, H), 1) // 4 == iota((R, H), 0) // 4)
    pick = (iota((H, L), 0) % 4 == iota((H, L), 1) // 64).astype(f32)
    return jnp.dot(
        jnp.where(keep, jnp.broadcast_to(q_row, (R, H)), 0.0), pick, precision=highest, preferred_element_type=f32
    )


def levels_kernel(thick, wet, rho, te, tn, prefix, force_e, force_n, depth, run, acc):
    step = pl.program_id(0)

    @pl.when(step == 0)
    def _():
        run[...] = jnp.zeros((R, L), f32)
        acc[...] = jnp.zeros((R, L), f32)
        force_e[...] = jnp.zeros((R, L), f32)
        force_n[...] = jnp.zeros((R, L), f32)
        depth[...] = jnp.zeros((R, L), f32)

    own = wet[...]
    p = run[...]
    g = acc[...]
    fe = force_e[...]
    fn = force_n[...]
    d = depth[...]
    for i in range(KB):
        k = step * KB + i
        t = thick[k]
        p = p + t * rho[i]
        g = g + t * p
        prefix[i] = g
        ta = jnp.where(own > k.astype(f32), t, 0.0)
        d = d + ta
        fe = fe + ta * te[i]
        fn = fn + ta * tn[i]
    run[...] = p
    acc[...] = g
    force_e[...] = fe
    force_n[...] = fn
    depth[...] = d


def edges_kernel(prefix, wet, wet_e, wet_w, wet_n, wet_s, te, tn, depth, x0,
                 fe_out, fn_out, oe, ow, on, os_, pe, pw, pn, ps, m8, a8):
    own = wet[...]
    lane = iota((R, L), 1)
    row = iota((R, L), 0)
    we = jnp.concatenate([wet_e[...], wet_e[...]], axis=1)
    ww = jnp.concatenate([wet_w[...], wet_w[...]], axis=1)
    wn = jnp.concatenate([wet_n[...], wet_n[...]], axis=0)
    ws = jnp.concatenate([wet_s[...], wet_s[...]], axis=0)
    for d, n in enumerate((1, 2)):
        m8[d] = jnp.minimum(own, jnp.where(lane >= L - n, pltpu.roll(we, L - n, 1), pltpu.roll(own, L - n, 1)))
        m8[2 + d] = jnp.minimum(own, jnp.where(lane < n, pltpu.roll(ww, n, 1), pltpu.roll(own, n, 1)))
        m8[4 + d] = jnp.minimum(own, jnp.where(row >= R - n, pltpu.roll(wn, R - n, 0), pltpu.roll(own, R - n, 0)))
        m8[6 + d] = jnp.minimum(own, jnp.where(row < n, pltpu.roll(ws, n, 0), pltpu.roll(own, n, 0)))
    for a in range(2):
        for b in range(2):
            rs, ls = slice(8 * a, 8 * a + 8), slice(H * b, H * b + H)
            m = [m8[i, rs, ls] for i in range(8)]
            acc = [jnp.zeros((8, H), f32)] * 8
            for k in range(K):
                g = prefix[k, rs, ls]
                acc = [jnp.where(mi > float(k), g, ai) for mi, ai in zip(m, acc)]
            for i in range(8):
                a8[i, rs, ls] = acc[i]
    e1 = pltpu.roll(a8[0], 1, 1) * (8.0 / 12.0)
    e2 = pltpu.roll(a8[1], 2, 1) * (1.0 / 12.0)
    w1 = pltpu.roll(a8[2], L - 1, 1) * (8.0 / 12.0)
    w2 = pltpu.roll(a8[3], L - 2, 1) * (1.0 / 12.0)
    n1 = pltpu.roll(a8[4], 1, 0) * (8.0 / 12.0)
    n2 = pltpu.roll(a8[5], 2, 0) * (1.0 / 12.0)
    s1 = pltpu.roll(a8[6], R - 1, 0) * (8.0 / 12.0)
    s2 = pltpu.roll(a8[7], R - 2, 0) * (1.0 / 12.0)

    def part(one, two, far1, far2, outside):
        if outside:
            return jnp.where(far1, one, 0.0) - jnp.where(far2, two, 0.0)
        return jnp.where(far1, 0.0, one) - jnp.where(far2, 0.0, two)

    fe = te[...] + part(e1, e2, lane < 1, lane < 2, False) - part(w1, w2, lane >= L - 1, lane >= L - 2, False)
    fn = tn[...] + part(n1, n2, row < 1, row < 2, False) - part(s1, s2, row >= R - 1, row >= R - 2, False)
    out_e = part(e1, e2, lane < 1, lane < 2, True)
    out_w = -part(w1, w2, lane >= L - 1, lane >= L - 2, True)
    out_n = part(n1, n2, row < 1, row < 2, True)
    out_s = -part(s1, s2, row >= R - 1, row >= R - 2, True)
    fe_out[...] = fe
    fn_out[...] = fn
    oe[...] = out_e[:, :H]
    ow[...] = out_w[:, H:]
    on[...] = out_n[:8]
    os_[...] = out_s[8:]
    d = depth[...]
    x = x0[...]
    lane_t = iota((R, H), 1)
    row_t = iota((8, L), 0)
    pe[:R] = jnp.where(lane_t < 2, out_e[:, :H], fe[:, H:])
    pe[R:] = jnp.where(lane_t == H - 1, d[:, H:], pltpu.roll(x[:, H:], H - 1, 1))
    pw[:R] = jnp.where(lane_t >= H - 2, out_w[:, H:], fe[:, :H])
    pw[R:] = jnp.where(lane_t == 0, d[:, :H], pltpu.roll(x[:, :H], 1, 1))
    pn[:8] = jnp.where(row_t < 2, out_n[:8], fn[8:])
    pn[8:] = jnp.where(row_t == 7, d[8:], pltpu.roll(x[8:], 7, 0))
    ps[:8] = jnp.where(row_t >= 6, out_s[8:], fn[:8])
    ps[8:] = jnp.where(row_t == 0, d[:8], pltpu.roll(x[:8], 1, 0))


def residual_kernel(fe_in, fn_in, oe, ow, on, os_, ge, gw, gn, gs, wet, depth, x0,
                    res, scaled, faces, pay, lo_ref=None):
    lane = iota((R, L), 1)
    row = iota((R, L), 0)
    zt = jnp.zeros((R, H), f32)
    zr = jnp.zeros((8, L), f32)
    wide_w = jnp.concatenate([gw[:R], zt], axis=1)
    wide_e = jnp.concatenate([zt, ge[:R]], axis=1)
    tall_s = jnp.concatenate([gs[:8], zr], axis=0)
    tall_n = jnp.concatenate([zr, gn[:8]], axis=0)
    fe = fe_in[...] + jnp.where(lane < 2, wide_w, 0.0) + jnp.where(lane >= L - 2, wide_e, 0.0)
    fn = fn_in[...] + jnp.where(row < 2, tall_s, 0.0) + jnp.where(row >= R - 2, tall_n, 0.0)
    fe_w = gw[:R, H - 1 :] + ow[:, H - 1 :]
    fe_e = ge[:R, :1] + oe[:, :1]
    fn_s = gs[7:8] + os_[7:8]
    fn_n = gn[0:1] + on[0:1]
    d_w, x_w = gw[R:, H - 1 :], gw[R:, H - 2 : H - 1]
    d_e, x_e = ge[R:, :1], ge[R:, 1:2]
    d_s, x_s = gs[15:16], gs[14:15]
    d_n, x_n = gn[8:9], gn[9:10]
    mask = (wet[...] > 0.0).astype(f32)
    d = depth[...]
    face_e = jnp.minimum(d, east(d, d_e))
    face_w = jnp.minimum(d, west(d, d_w))
    face_n = jnp.minimum(d, north(d, d_n))
    face_s = jnp.minimum(d, south(d, d_s))
    diag = mask * (EPS + face_e + face_w + face_n + face_s) + (1.0 - mask)
    x = x0[...]
    ax = diag * x - (
        face_e * east(x, x_e) + face_w * west(x, x_w) + face_n * north(x, x_n) + face_s * south(x, x_s)
    )
    r = mask * 0.5 * (west(fe, fe_w) - east(fe, fe_e) + south(fn, fn_s) - north(fn, fn_n)) - ax
    s = r / diag
    res[...] = r
    scaled[...] = s
    faces[0] = face_e
    faces[1] = face_w
    faces[2] = face_n
    faces[3] = face_s
    faces[4] = diag
    (w,) = tile_sums([r * mask])
    pay[...] = pack([w], lax.axis_index("lon") % 8)


def apply_faces(faces, v, ve, vw, vn, vs):
    return faces[4] * v - (
        faces[0] * east(v, ve) + faces[1] * west(v, vw) + faces[2] * north(v, vn) + faces[3] * south(v, vs)
    )


def first_kernel(got, coarse, res, scaled, faces, wet, se, sw, sn, ss, w_out, as_out, pay):
    w = jnp.sum(got[...].reshape(NDEV // 8, 8, H), axis=1)
    w_out[...] = w
    q = coarse_rows(coarse, w)
    s = scaled[...]
    mask = (wet[...] > 0.0).astype(f32)
    a_s = apply_faces(faces, s, se[:, :1], sw[:, H - 1 :], sn[0:1], ss[7:8])
    as_out[...] = a_s
    sums = tile_sums([
        a_s * mask,
        mask,
        jnp.where(iota((R, L), 1) % 64 == 63, faces[0], 0.0),
        jnp.where(iota((R, L), 0) % 4 == 3, faces[2], 0.0),
        s * a_s,
        res[...] * s,
    ])
    pay[...] = pack([q] + sums, lax.axis_index("lon") % 8)


def step_kernel(got, w_in, res, scaled, a_s, faces, wet, wet_e, wet_w, wet_n, wet_s, se, sw, sn, ss, x0,
                r_out, s_out, x_out, d_out, ad_out, w_out, u_out, net_out, num_out):
    g = got[...]
    q, a, count, link_e, link_n, cc, ee = [unpack(g, f) for f in range(7)]
    w = w_in[...]
    tq = coarse_operator(q, count, link_e, link_n)
    u = a + tq
    d_a_d = total(cc + q * (2.0 * a + tq))
    rz = total(ee + w * q)
    alpha = rz / d_a_d
    w_out[...] = w - alpha * u
    u_out[...] = u
    net_out[0] = count
    net_out[1] = link_e
    net_out[2] = link_n
    num_out[0:1] = jnp.broadcast_to(rz, (1, H))
    num_out[1:2] = jnp.broadcast_to(d_a_d, (1, H))
    num_out[2:] = jnp.zeros((6, H), f32)
    mask = (wet[...] > 0.0).astype(f32)
    pq, pe, pw, pn, ps = spread(got, lax.axis_index("lat"), lax.axis_index("lon"))
    pq = pq * mask
    pe = jnp.where(wet_e[:, :1] > 0.0, pe, 0.0)
    pw = jnp.where(wet_w[:, H - 1 :] > 0.0, pw, 0.0)
    pn = jnp.where(wet_n[0:1] > 0.0, pn, 0.0)
    ps = jnp.where(wet_s[7:8] > 0.0, ps, 0.0)
    d = scaled[...] + pq
    ad = a_s[...] + apply_faces(faces, pq, pe, pw, pn, ps)
    r = res[...] - alpha * ad
    r_out[...] = r
    s_out[...] = r / faces[4]
    x_out[...] = x0[...] + alpha * d
    d_out[...] = d
    ad_out[...] = ad


def product_kernel(coarse, w, q_out):
    q_out[...] = jnp.broadcast_to(coarse_rows(coarse, w[...]), (8, H))


def second_kernel(q, res, scaled, ad, faces, wet, se, sw, sn, ss, as_out, pay):
    s = scaled[...]
    mask = (wet[...] > 0.0).astype(f32)
    a_s = apply_faces(faces, s, se[:, :1], sw[:, H - 1 :], sn[0:1], ss[7:8])
    as_out[...] = a_s
    sums = tile_sums([a_s * mask, s * a_s, res[...] * s, s * ad[...]])
    pay[...] = pack([q[0:1]] + sums, lax.axis_index("lon") % 8)


def last_kernel(got, w_in, u_in, net, num, coarse, res, scaled, a_s, ad, d_in, x_in, faces,
                wet, wet_e, wet_w, wet_n, wet_s, surface, precond):
    g = got[...]
    q, a, cc, ee, hh = [unpack(g, f) for f in range(5)]
    w = w_in[...]
    u0 = u_in[...]
    rz0 = num[0:1, :1]
    dad0 = num[1:2, :1]
    tq = coarse_operator(q, net[0], net[1], net[2])
    zaz = total(cc + q * (2.0 * a + tq))
    rz = total(ee + w * q)
    zad = total(hh + q * u0)
    beta = rz / rz0
    alpha = rz / (zaz + 2.0 * beta * zad + beta * beta * dad0)
    w2 = w - alpha * (a + tq + beta * u0)
    q2 = prolong_row(coarse_rows(coarse, w2))
    mask = (wet[...] > 0.0).astype(f32)
    pq, pe, pw, pn, ps = spread(got, lax.axis_index("lat"), lax.axis_index("lon"))
    pq = pq * mask
    pe = jnp.where(wet_e[:, :1] > 0.0, pe, 0.0)
    pw = jnp.where(wet_w[:, H - 1 :] > 0.0, pw, 0.0)
    pn = jnp.where(wet_n[0:1] > 0.0, pn, 0.0)
    ps = jnp.where(wet_s[7:8] > 0.0, ps, 0.0)
    d = scaled[...] + pq + beta * d_in[...]
    ad1 = a_s[...] + apply_faces(faces, pq, pe, pw, pn, ps) + beta * ad[...]
    surface[...] = x_in[...] + alpha * d
    precond[...] = (res[...] - alpha * ad1) / faces[4] + q2 * mask


def to_east(v):
    return lax.ppermute(v, "lon", [(i, (i + 1) % NLON) for i in range(NLON)])


def to_west(v):
    return lax.ppermute(v, "lon", [((i + 1) % NLON, i) for i in range(NLON)])


def to_north(v):
    return lax.ppermute(v, "lat", [(i, i + 1) for i in range(NLAT - 1)])


def to_south(v):
    return lax.ppermute(v, "lat", [(i + 1, i) for i in range(NLAT - 1)])


def swap(e, w, n, s):
    return to_west(w), to_east(e), to_south(s), to_north(n)


def edges_of(v):
    return swap(v[:, H:], v[:, :H], v[8:], v[:8])


def gather(pay):
    return lax.all_to_all(pay, BOTH, 0, 0, tiled=True)


def body(density, tend_east, tend_north, thickness, levels, ocean_mask, eta_prev, coarse):
    wet = (levels * ocean_mask).astype(f32)
    x0 = ocean_mask.astype(f32) * eta_prev
    wet_e, wet_w, wet_n, wet_s = edges_of(wet)
    plane = (R, L)
    level_block = pl.BlockSpec((KB, R, L), lambda i: (i, 0, 0))
    fixed = pl.BlockSpec(plane, lambda i: (0, 0))
    prefix, te, tn, depth = pl.pallas_call(
        levels_kernel,
        grid=(K // KB,),
        in_specs=[pl.BlockSpec(memory_space=pltpu.SMEM), fixed, level_block, level_block, level_block],
        out_specs=[level_block, fixed, fixed, fixed],
        out_shape=[jax.ShapeDtypeStruct(s, f32) for s in ((K, R, L), plane, plane, plane)],
        scratch_shapes=[pltpu.VMEM(plane, f32), pltpu.VMEM(plane, f32)],
        name="levels",
    )(thickness, wet, density, tend_east, tend_north)
    tall, flat = (R, H), (8, L)
    out = call(
        edges_kernel,
        [plane, plane, tall, tall, flat, flat, (2 * R, H), (2 * R, H), (R, L), (R, L)],
        "edges",
        scratch_shapes=[pltpu.VMEM((8, R, L), f32), pltpu.VMEM((8, R, L), f32)],
    )(prefix, wet, wet_e, wet_w, wet_n, wet_s, te, tn, depth, x0)
    fe, fn, oe, ow, on, os_ = out[:6]
    ge, gw, gn, gs = swap(*out[6:])
    r0, s0, faces, pay = call(
        residual_kernel, [plane, plane, (5, R, L), (NDEV, H)], "residual"
    )(fe, fn, oe, ow, on, os_, ge, gw, gn, gs, wet, depth, x0)
    near = edges_of(s0)
    got = gather(pay)
    w0, as0, pay = call(first_kernel, [G, plane, (NDEV, H)], "first")(
        got, coarse, r0, s0, faces, wet, *near
    )
    got = gather(pay)
    r1, s1, x1, d0, ad0, w1, u0, net, num = call(
        step_kernel, [plane] * 5 + [G, G, (3,) + G, (8, H)], "step"
    )(got, w0, r0, s0, as0, faces, wet, wet_e, wet_w, wet_n, wet_s, *near, x0)
    near = edges_of(s1)
    (q1,) = call(product_kernel, [(8, H)], "product")(coarse, w1)
    as1, pay = call(second_kernel, [plane, (NDEV, H)], "second")(q1, r1, s1, ad0, faces, wet, *near)
    got = gather(pay)
    return tuple(
        call(last_kernel, [plane, plane], "last")(
            got, w1, u0, net, num, coarse, r1, s1, as1, ad0, d0, x1, faces, wet, wet_e, wet_w, wet_n, wet_s
        )
    )


def solution(mesh):
    return jax.shard_map(
        body,
        mesh=mesh,
        in_specs=(
            P(None, "lat", "lon"),
            P(None, "lat", "lon"),
            P(None, "lat", "lon"),
            P(),
            P("lat", "lon"),
            P("lat", "lon"),
            P("lat", "lon"),
            P(("lat", "lon"), None),
        ),
        out_specs=(P("lat", "lon"), P("lat", "lon")),
        check_vma=False,
    )
```

```python
import jax
import jax.numpy as jnp
from jax import lax
from jax.experimental import pallas as pl
from jax.experimental.pallas import tpu as pltpu
from jax.sharding import PartitionSpec as P

K = 75
KB = 15
R = 16
L = 256
H = 128
NLON = 16
NLAT = 16
NDEV = 256
EPS = 0.25
f32 = jnp.float32
highest = lax.Precision.HIGHEST
BOTH = ("lat", "lon")


def iota(shape, dim):
    return lax.broadcasted_iota(jnp.int32, shape, dim)


def in_vmem(shape):
    return pltpu.VMEM(shape, f32)


def call(kernel, out_shapes, out=in_vmem, **kw):
    vm = pl.BlockSpec(memory_space=pltpu.VMEM)

    def run(*args):
        return pl.pallas_call(
            kernel,
            out_shape=[out(s) for s in out_shapes],
            in_specs=[vm] * len(args),
            out_specs=[vm] * len(out_shapes),
            **kw,
        )(*[pltpu.with_memory_space_constraint(a, pltpu.VMEM) for a in args])

    return run


RX = R + 16
LX = L + 2 * H
ROWS = slice(8, 8 + R)
COLS = slice(H, H + L)


def beyond(v, rows, cols):
    n, m = v.shape
    if rows:
        v = pltpu.roll(v, -rows % n, 0)
    if cols:
        v = pltpu.roll(v, -cols % m, 1)
    return v


def apply_faces(faces, v):
    return faces[4] * v - (
        faces[0] * beyond(v, 0, 1)
        + faces[1] * beyond(v, 0, -1)
        + faces[2] * beyond(v, 1, 0)
        + faces[3] * beyond(v, -1, 0)
    )


def tile_sums(fields):
    n = len(fields)
    pick = (iota((L, H), 0) // 64 == iota((L, H), 1) % 4).astype(f32)
    cols = jnp.dot(jnp.concatenate(fields, axis=0), pick, precision=highest, preferred_element_type=f32)
    keep = iota((R, H), 0) // 4 == (iota((R, H), 1) % 16) // 4
    return [
        jnp.sum(jnp.where(keep, cols[R * i : R * i + R], 0.0), axis=0, keepdims=True)
        for i in range(n)
    ]


def pack(rows, rho):
    block = iota((1, H), 1) // 16
    out = jnp.zeros((1, H), f32)
    for f, row in enumerate(rows):
        out = jnp.where(block == (f + rho) % 8, row, out)
    return out


def unpack(got, f):
    shape = (NDEV // 8, 8, H)
    keep = iota(shape, 2) // 16 == (iota(shape, 1) + f) % 8
    flat = jnp.sum(jnp.where(keep, got.reshape(shape), 0.0), axis=1)
    return pltpu.roll(flat, (H - 16 * f) % H, 1) if f else flat


def coarse_rows(c_ref, w):
    acc = jnp.zeros((R, H), f32)
    for r in range(NDEV // 8):
        acc = acc + c_ref[:, H * r : H * r + H] * w[r : r + 1, :]
    col = jnp.sum(acc, axis=1, keepdims=True)
    return jnp.sum(jnp.where(iota((R, H), 0) == iota((R, H), 1) % 16, col, 0.0), axis=0, keepdims=True)


G = (NDEV // 8, H)


def c_east(q):
    lane = iota(G, 1)
    near = pltpu.roll(q, H - 1, 1)
    far = pltpu.roll(q, H - 13, 1)
    swap = jnp.where(iota(G, 0) % 2 == 0, pltpu.roll(far, G[0] - 1, 0), pltpu.roll(far, 1, 0))
    far = jnp.where(lane // 16 == 7, swap, far)
    return jnp.where(lane % 4 == 3, far, near)


def c_west(q):
    lane = iota(G, 1)
    near = pltpu.roll(q, 1, 1)
    far = pltpu.roll(q, 13, 1)
    swap = jnp.where(iota(G, 0) % 2 == 0, pltpu.roll(far, G[0] - 1, 0), pltpu.roll(far, 1, 0))
    far = jnp.where(lane // 16 == 0, swap, far)
    return jnp.where(lane % 4 == 0, far, near)


def c_north(q):
    near = pltpu.roll(q, H - 4, 1)
    far = pltpu.roll(pltpu.roll(q, 12, 1), G[0] - 2, 0)
    return jnp.where((iota(G, 1) % 16) // 4 == 3, far, near)


def c_south(q):
    near = pltpu.roll(q, 4, 1)
    far = pltpu.roll(pltpu.roll(q, H - 12, 1), 2, 0)
    return jnp.where((iota(G, 1) % 16) // 4 == 0, far, near)


def coarse_operator(q, count, link_e, link_n):
    flux_e = link_e * (q - c_east(q))
    flux_n = link_n * (q - c_north(q))
    return EPS * count * q + (flux_e - c_west(flux_e)) + (flux_n - c_south(flux_n))


def total(v):
    return jnp.sum(jnp.sum(v, axis=0, keepdims=True), axis=1, keepdims=True)


def neighbour(la, lo, da, do):
    a = la + da
    there = jnp.logical_and(a >= 0, a < NLAT)
    a = jnp.clip(a, 0, NLAT - 1)
    return a * NLON + (lo + do + NLON) % NLON, there


def lane_column(row, f, o):
    lane = iota((R, H), 1)
    hit = (lane // 16 == (f + o) % 8) & (lane % 16 == iota((R, H), 0))
    return jnp.sum(jnp.where(hit, jnp.broadcast_to(row, (R, H)), 0.0), axis=1, keepdims=True)


def lane_value(row, f, o):
    hit = iota((1, H), 1) == 16 * ((f + o) % 8)
    return jnp.sum(jnp.where(hit, row, 0.0), axis=1, keepdims=True)


def column_lanes(v, c):
    return jnp.sum(
        jnp.where(iota((R, H), 0) == iota((R, H), 1) % 16, v[:, c : c + 1], 0.0), axis=0, keepdims=True
    )


def spread(got_ref, la, lo):
    row = iota((RX, H), 0)
    lane = iota((RX, H), 1)
    ty = jnp.where(row < 8, 3, jnp.where(row < 8 + R, (row - 8) // 4, 0))
    src = jnp.zeros((RX, H), f32)
    l2 = iota((H, LX), 0)
    c2 = iota((H, LX), 1)
    pick = jnp.zeros((H, LX), f32)
    for do in (-1, 0, 1):
        o = (lo + do + NLON) % NLON
        south, mine, north = [
            jnp.broadcast_to(got_ref[pl.ds(neighbour(la, lo, da, do)[0], 1), :], (RX, H)) for da in (-1, 0, 1)
        ]
        part = jnp.where(row < 8, south, jnp.where(row < 8 + R, mine, north))
        src = jnp.where((lane // 16 == o % 8) & ((lane % 16) // 4 == ty), part, src)
        if do == 0:
            to = (c2 >= H) & (c2 < H + L) & (l2 % 4 == (c2 - H) // 64)
        elif do < 0:
            to = (c2 < H) & (l2 % 4 == 3)
        else:
            to = (c2 >= H + L) & (l2 % 4 == 0)
        pick = jnp.where(to & (l2 // 16 == o % 8), 1.0, pick)
    return jnp.dot(src, pick, precision=highest, preferred_element_type=f32)


def prolong_row(q_row):
    keep = (iota((R, H), 1) < 16) & (iota((R, H), 1) // 4 == iota((R, H), 0) // 4)
    pick = (iota((H, L), 0) % 4 == iota((H, L), 1) // 64).astype(f32)
    return jnp.dot(
        jnp.where(keep, jnp.broadcast_to(q_row, (R, H)), 0.0), pick, precision=highest, preferred_element_type=f32
    )


CHUNKS = K // KB
NEAR = 0
FAR = 80
M_FORCE, M_WET1, M_WET2, M_DEPTH1, M_DEPTH2, M_X = range(6)
LAT_MISC = 160
LAT_ROWS = 168
LON_MISC = 2 * K
LON_LANES = 2 * H


def levels_kernel(thick, levels, mask, eta, rho, te, tn,
                  fe_out, fn_out, wet_out, x_out, depth_out, pe, pw, pn, ps,
                  t_s, lev_v, mask_v, eta_v, rho_v, te_v, tn_v, m8, a8, run, sem):
    small = [
        pltpu.make_async_copy(a, b, sem.at[3 * CHUNKS + i])
        for i, (a, b) in enumerate(((thick, t_s), (levels, lev_v), (mask, mask_v), (eta, eta_v)))
    ]
    for c in small:
        c.start()
    big = []
    for c in range(CHUNKS):
        part = pl.ds(c * KB, KB)
        big.append([
            pltpu.make_async_copy(a.at[part], b.at[part], sem.at[3 * c + i])
            for i, (a, b) in enumerate(((rho, rho_v), (te, te_v), (tn, tn_v)))
        ])
        for x in big[-1]:
            x.start()
    for c in small:
        c.wait()
    own = (lev_v[...] * mask_v[...]).astype(f32)
    wet_out[...] = own
    x_out[...] = mask_v[...].astype(f32) * eta_v[...]
    lane = iota((R, L), 1)
    row = iota((R, L), 0)
    for d, n in enumerate((1, 2)):
        m8[d] = jnp.where(lane < L - n, jnp.minimum(own, beyond(own, 0, n)), 0.0)
        m8[2 + d] = jnp.where(lane >= n, jnp.minimum(own, beyond(own, 0, -n)), 0.0)
        m8[4 + d] = jnp.where(row < R - n, jnp.minimum(own, beyond(own, n, 0)), 0.0)
        m8[6 + d] = jnp.where(row >= n, jnp.minimum(own, beyond(own, -n, 0)), 0.0)
    zero = jnp.zeros((8, H), f32)
    lane8 = iota((8, H), 1)
    for c in range(CHUNKS):
        for x in big[c]:
            x.wait()
        for a in range(2):
            for b in range(2):
                rs, ls = slice(8 * a, 8 * a + 8), slice(H * b, H * b + H)
                m = [m8[i, rs, ls] for i in range(8)]
                wet = wet_out[rs, ls]
                if c == 0:
                    p = g = d = fe = fn = zero
                    acc = [zero] * 8
                    prof = [zero, zero]
                else:
                    p, g = run[0, rs, ls], run[1, rs, ls]
                    d, fe, fn = depth_out[rs, ls], fe_out[rs, ls], fn_out[rs, ls]
                    acc = [a8[i, rs, ls] for i in range(8)]
                    lon_out = pe if b else pw
                    prof = [lon_out[rs, :H], lon_out[rs, H:]]
                for k in range(c * KB, c * KB + KB):
                    t = t_s[k]
                    p = p + t * rho_v[k, rs, ls]
                    g = g + t * p
                    ta = jnp.where(wet > float(k), t, 0.0)
                    d = d + ta
                    fe = fe + ta * te_v[k, rs, ls]
                    fn = fn + ta * tn_v[k, rs, ls]
                    acc = [jnp.where(mi > float(k), g, ai) for mi, ai in zip(m, acc)]
                    h, at = (2 * k) // H, (2 * k) % H
                    moved = pltpu.roll(g, (at + 2) % H if b else at, 1) if (at + 2 * b) % H else g
                    prof[h] = jnp.where((lane8 == at) | (lane8 == at + 1), moved, prof[h])
                    lat_out = pn if a else ps
                    near, far = (7, 6) if a else (0, 1)
                    lat_out[NEAR + k : NEAR + k + 1, ls] = g[near : near + 1]
                    lat_out[FAR + k : FAR + k + 1, ls] = g[far : far + 1]
                if c + 1 < CHUNKS:
                    run[0, rs, ls] = p
                    run[1, rs, ls] = g
                depth_out[rs, ls] = d
                fe_out[rs, ls] = fe
                fn_out[rs, ls] = fn
                for i in range(8):
                    a8[i, rs, ls] = acc[i]
                lon_out = pe if b else pw
                lon_out[rs, :H] = prof[0]
                lon_out[rs, H:] = prof[1]
    c1, c2 = 8.0 / 12.0, 1.0 / 12.0
    fe = fe_out[...] + c1 * (beyond(a8[0], 0, -1) - beyond(a8[2], 0, 1)) - c2 * (
        beyond(a8[1], 0, -2) - beyond(a8[3], 0, 2)
    )
    fn = fn_out[...] + c1 * (beyond(a8[4], -1, 0) - beyond(a8[6], 1, 0)) - c2 * (
        beyond(a8[5], -2, 0) - beyond(a8[7], 2, 0)
    )
    fe_out[...] = fe
    fn_out[...] = fn
    d = depth_out[...]
    x = x_out[...]
    lane_t = iota((R, H), 1)

    def lon_misc(out, force, wet, dep, xs, near, far):
        tile = out[:, H:]
        for i, (v, at) in enumerate(((force, near), (wet, near), (wet, far), (dep, near), (dep, far), (xs, near))):
            to = LON_MISC - H + i
            tile = jnp.where(lane_t == to, pltpu.roll(v, (to - at) % H, 1), tile)
        out[:, H:] = tile

    lon_misc(pe, fe[:, H:], own[:, H:], d[:, H:], x[:, H:], H - 1, H - 2)
    lon_misc(pw, fe[:, :H], own[:, :H], d[:, :H], x[:, :H], 0, 1)
    for out, near, far in ((pn, R - 1, R - 2), (ps, 0, 1)):
        for i, (v, at) in enumerate(((fn, near), (own, near), (own, far), (d, near), (d, far), (x, near))):
            out[LAT_MISC + i : LAT_MISC + i + 1] = v[at : at + 1]


def residual_kernel(fe_in, fn_in, wet, x0, depth, pe, pw, pn, ps, ge, gw, gn, gs,
                    res, scaled, dep_x, rows_n, rows_s, pay):
    own = wet[...]
    lane = iota((R, L), 1)
    row = iota((R, L), 0)

    def lon_misc(ref, i):
        return ref[:, LON_MISC + i : LON_MISC + i + 1]

    la, lo = lax.axis_index("lat"), lax.axis_index("lon")

    def lat_misc(ref, i):
        there = la < NLAT - 1 if ref is gn else la > 0
        return jnp.where(there, ref[LAT_MISC + i : LAT_MISC + i + 1], 0.0)

    def lon_pick(ref, m, col):
        at = 2 * m.astype(jnp.int32) - 2 + col
        return jnp.sum(jnp.where((lane == at) & (m > 0.0), ref[...], 0.0), axis=1, keepdims=True)

    level = iota((FAR, L), 0).astype(f32) + 1.0

    def lat_pick(ref, m, col):
        part = ref[FAR : 2 * FAR] if col else ref[NEAR : NEAR + FAR]
        return jnp.sum(jnp.where(level == m, part, 0.0), axis=0, keepdims=True)

    def cross(pick, got, sent, o1, o2, n1, n2, got_near, sent_near):
        gn_, sn_ = (0, 1) if got_near == 0 else (1, 0), (0, 1) if sent_near == 0 else (1, 0)
        first = (-8.0 * pick(got, jnp.minimum(o1, n1), gn_[0]) + pick(got, jnp.minimum(o1, n2), gn_[1])) / 12.0
        second = pick(got, jnp.minimum(o2, n1), gn_[0]) / 12.0
        theirs = (8.0 * pick(sent, jnp.minimum(n1, o1), sn_[0]) - pick(sent, jnp.minimum(n1, o2), sn_[1])) / 12.0
        return first, second, theirs

    fe = fe_in[...]
    fn = fn_in[...]
    a, b, far_e = cross(lon_pick, ge, pe, own[:, L - 1 :], own[:, L - 2 : L - 1],
                        lon_misc(ge, M_WET1), lon_misc(ge, M_WET2), 0, 1)
    fe = fe + jnp.where(lane == L - 1, a, 0.0) + jnp.where(lane == L - 2, b, 0.0)
    fe_e = lon_misc(ge, M_FORCE) + far_e
    a, b, far_w = cross(lon_pick, gw, pw, own[:, :1], own[:, 1:2],
                        lon_misc(gw, M_WET1), lon_misc(gw, M_WET2), 1, 0)
    fe = fe - jnp.where(lane == 0, a, 0.0) - jnp.where(lane == 1, b, 0.0)
    fe_w = lon_misc(gw, M_FORCE) - far_w
    a, b, far_n = cross(lat_pick, gn, pn, own[R - 1 :], own[R - 2 : R - 1],
                        lat_misc(gn, M_WET1), lat_misc(gn, M_WET2), 0, 0)
    fn = fn + jnp.where(row == R - 1, a, 0.0) + jnp.where(row == R - 2, b, 0.0)
    fn_n = lat_misc(gn, M_FORCE) + far_n
    a, b, far_s = cross(lat_pick, gs, ps, own[:1], own[1:2],
                        lat_misc(gs, M_WET1), lat_misc(gs, M_WET2), 0, 0)
    fn = fn - jnp.where(row == 0, a, 0.0) - jnp.where(row == 1, b, 0.0)
    fn_s = lat_misc(gs, M_FORCE) - far_s

    def shifts(v, e, w, n, s):
        return (
            jnp.where(lane == L - 1, e, beyond(v, 0, 1)),
            jnp.where(lane == 0, w, beyond(v, 0, -1)),
            jnp.where(row == R - 1, n, beyond(v, 1, 0)),
            jnp.where(row == 0, s, beyond(v, -1, 0)),
        )

    mask = (own > 0.0).astype(f32)
    d = depth[...]
    x = x0[...]
    face = [
        jnp.minimum(d, v)
        for v in shifts(d, lon_misc(ge, M_DEPTH1), lon_misc(gw, M_DEPTH1), lat_misc(gn, M_DEPTH1), lat_misc(gs, M_DEPTH1))
    ]
    diag = mask * (EPS + face[0] + face[1] + face[2] + face[3]) + (1.0 - mask)
    ax = diag * x
    for f, v in zip(face, shifts(x, lon_misc(ge, M_X), lon_misc(gw, M_X), lat_misc(gn, M_X), lat_misc(gs, M_X))):
        ax = ax - f * v
    f_e, f_w, _, _ = shifts(fe, fe_e, fe_w, fn_n, fn_s)
    _, _, f_n, f_s = shifts(fn, fe_e, fe_w, fn_n, fn_s)
    r = mask * 0.5 * (f_w - f_e + f_s - f_n) - ax
    s = r / diag
    res[...] = r
    scaled[...] = s
    rows_n[...] = s[8:]
    rows_s[...] = s[:8]
    dep_x[...] = jnp.zeros((RX, LX), f32)
    dep_x[ROWS, COLS] = d
    dep_x[7:8, COLS] = lat_misc(gs, M_DEPTH1)
    dep_x[6:7, COLS] = lat_misc(gs, M_DEPTH2)
    dep_x[8 + R : 9 + R, COLS] = lat_misc(gn, M_DEPTH1)
    dep_x[9 + R : 10 + R, COLS] = lat_misc(gn, M_DEPTH2)
    lane_t = iota((R, H), 1)
    dep_x[ROWS, :H] = jnp.where(
        lane_t == H - 1, lon_misc(gw, M_DEPTH1), jnp.where(lane_t == H - 2, lon_misc(gw, M_DEPTH2), 0.0)
    )
    dep_x[ROWS, H + L :] = jnp.where(
        lane_t == 0, lon_misc(ge, M_DEPTH1), jnp.where(lane_t == 1, lon_misc(ge, M_DEPTH2), 0.0)
    )
    rho = lo % 8
    (w,) = tile_sums([r * mask])
    pay[...] = jnp.broadcast_to(pack([w], rho), (NDEV, H))
    for do, c1, c2 in ((1, L - 1, L - 2), (-1, 0, 1)):
        at, _ = neighbour(la, lo, 0, do)
        pay[pl.ds(at, 1), :] = pack([w, column_lanes(s, c1), column_lanes(s, c2)], rho)
        for da, j in ((1, R - 1), (-1, 0)):
            at, there = neighbour(la, lo, da, do)
            at = jnp.where(there, at, la * NLON + lo)
            pay[pl.ds(at, 1), :] = pack(
                [w, jnp.broadcast_to(s[j : j + 1, c1 : c1 + 1], (1, H)), jnp.broadcast_to(d[j : j + 1, c1 : c1 + 1], (1, H))],
                rho,
            )


def first_kernel(got, coarse, res, scaled, dep_in, sn, ss, w_out, s_x, faces, pay):
    la, lo = lax.axis_index("lat"), lax.axis_index("lon")
    w = unpack(got[...], 0)
    w_out[...] = w
    q = coarse_rows(coarse, w)
    s = scaled[...]
    s_x[ROWS, COLS] = s
    s_x[:8, COLS] = jnp.where(la > 0, ss[...], 0.0)
    s_x[8 + R :, COLS] = jnp.where(la < NLAT - 1, sn[...], 0.0)
    lane = iota((R, H), 1)
    dep = dep_in[...]
    dep_x = faces.at[4]
    dep_x[...] = dep
    for do, cols, l1, l2 in ((1, slice(H + L, LX), 0, 1), (-1, slice(0, H), H - 1, H - 2)):
        at, _ = neighbour(la, lo, 0, do)
        o = (lo + do + NLON) % NLON
        msg = got[pl.ds(at, 1), :]
        s_x[ROWS, cols] = jnp.where(lane == l1, lane_column(msg, 1, o), jnp.where(lane == l2, lane_column(msg, 2, o), 0.0))
        for da, rows, j in ((1, slice(8 + R, RX), 0), (-1, slice(0, 8), 7)):
            at, there = neighbour(la, lo, da, do)
            msg = got[pl.ds(at, 1), :]
            here = (iota((8, H), 0) == j) & (iota((8, H), 1) == l1) & there
            s_x[rows, cols] = jnp.where(here, lane_value(msg, 1, o), 0.0)
            dep_x[rows, cols] = jnp.where(here, lane_value(msg, 2, o), 0.0)
    d = dep_x[...]
    mask = (d > 0.0).astype(f32)
    face = [jnp.minimum(d, beyond(d, a, b)) for a, b in ((0, 1), (0, -1), (1, 0), (-1, 0))]
    for i in range(4):
        faces[i] = face[i]
    diag = mask * (EPS + face[0] + face[1] + face[2] + face[3]) + (1.0 - mask)
    faces[4] = diag
    faces[5] = mask
    own = (ROWS, COLS)
    a_s = apply_faces(face + [diag], s_x[...])[own]
    sums = tile_sums([
        a_s * mask[own],
        mask[own],
        jnp.where(iota((R, L), 1) % 64 == 63, face[0][own], 0.0),
        jnp.where(iota((R, L), 0) % 4 == 3, face[2][own], 0.0),
        s * a_s,
        res[...] * s,
    ])
    pay[...] = jnp.broadcast_to(pack([q] + sums, lo % 8), (NDEV, H))


def step_kernel(got, coarse, w_in, res, s_x, faces, x0,
                r_out, s_out, as_out, x_out, d_out, ad_out, w_out, u_out, net_out, num_out, pay):
    la, lo = lax.axis_index("lat"), lax.axis_index("lon")
    own = (ROWS, COLS)
    g = got[...]
    q, a, count, link_e, link_n, cc, ee = [unpack(g, f) for f in range(7)]
    w = w_in[...]
    tq = coarse_operator(q, count, link_e, link_n)
    u = a + tq
    d_a_d = total(cc + q * (2.0 * a + tq))
    rz = total(ee + w * q)
    alpha = rz / d_a_d
    w = w - alpha * u
    w_out[...] = w
    u_out[...] = u
    net_out[0] = count
    net_out[1] = link_e
    net_out[2] = link_n
    num_out[0:1] = jnp.broadcast_to(rz, (1, H))
    num_out[1:2] = jnp.broadcast_to(d_a_d, (1, H))
    num_out[2:] = jnp.zeros((6, H), f32)
    q = coarse_rows(coarse, w)
    face = [faces[i] for i in range(6)]
    mask = face[5]
    s = s_x[...]
    d = s + mask * spread(got, la, lo)
    ad = apply_faces(face, d)
    s = s - alpha * (ad / face[4])
    a_s = apply_faces(face, s)[own]
    ad = ad[own]
    s = s[own]
    r = res[...] - alpha * ad
    r_out[...] = r
    s_out[...] = s
    as_out[...] = a_s
    x_out[...] = x0[...] + alpha * d[own]
    d_out[...] = d[own]
    ad_out[...] = ad
    sums = tile_sums([a_s * mask[own], s * a_s, r * s, s * ad])
    pay[...] = jnp.broadcast_to(pack([q] + sums, lo % 8), (NDEV, H))


def last_kernel(got, w_in, u_in, net, num, coarse, res, scaled, a_s, ad, d_in, x_in, faces, surface, precond):
    la, lo = lax.axis_index("lat"), lax.axis_index("lon")
    own = (ROWS, COLS)
    g = got[...]
    q, a, cc, ee, hh = [unpack(g, f) for f in range(5)]
    w = w_in[...]
    u0 = u_in[...]
    rz0 = num[0:1, :1]
    dad0 = num[1:2, :1]
    tq = coarse_operator(q, net[0], net[1], net[2])
    zaz = total(cc + q * (2.0 * a + tq))
    rz = total(ee + w * q)
    zad = total(hh + q * u0)
    beta = rz / rz0
    alpha = rz / (zaz + 2.0 * beta * zad + beta * beta * dad0)
    q2 = prolong_row(coarse_rows(coarse, w - alpha * (a + tq + beta * u0)))
    face = [faces[i] for i in range(6)]
    mask = face[5]
    pq = mask * spread(got, la, lo)
    d = scaled[...] + pq[own] + beta * d_in[...]
    ad1 = a_s[...] + apply_faces(face, pq)[own] + beta * ad[...]
    surface[...] = x_in[...] + alpha * d
    precond[...] = (res[...] - alpha * ad1) / face[4][own] + q2 * mask[own]


def to_east(v):
    return lax.ppermute(v, "lon", [(i, (i + 1) % NLON) for i in range(NLON)])


def to_west(v):
    return lax.ppermute(v, "lon", [((i + 1) % NLON, i) for i in range(NLON)])


def to_north(v):
    return lax.ppermute(v, "lat", [(i, (i + 1) % NLAT) for i in range(NLAT)])


def to_south(v):
    return lax.ppermute(v, "lat", [((i + 1) % NLAT, i) for i in range(NLAT)])


def gather(pay):
    return lax.all_to_all(pay, BOTH, 0, 0, tiled=True)


def body(density, tend_east, tend_north, thickness, levels, ocean_mask, eta_prev, coarse):
    plane, wide = (R, L), (RX, LX)
    lon_msg, lat_msg = (R, LON_LANES), (LAT_ROWS, L)
    vm = pl.BlockSpec(memory_space=pltpu.VMEM)
    fe, fn, wet, x0, depth, pe, pw, pn, ps = pl.pallas_call(
        levels_kernel,
        in_specs=[pl.BlockSpec(memory_space=pl.ANY)] * 7,
        out_specs=[vm] * 9,
        out_shape=[in_vmem(s) for s in [plane] * 5 + [lon_msg] * 2 + [lat_msg] * 2],
        scratch_shapes=[
            pltpu.SMEM((K,), f32),
            pltpu.VMEM(plane, jnp.int32),
            pltpu.VMEM(plane, jnp.int32),
            pltpu.VMEM(plane, f32),
            pltpu.VMEM((K, R, L), f32),
            pltpu.VMEM((K, R, L), f32),
            pltpu.VMEM((K, R, L), f32),
            pltpu.VMEM((8, R, L), f32),
            pltpu.VMEM((8, R, L), f32),
            pltpu.VMEM((2, R, L), f32),
            pltpu.SemaphoreType.DMA((3 * CHUNKS + 4,)),
        ],
        name="levels",
    )(thickness, levels, ocean_mask, eta_prev, density, tend_east, tend_north)
    gn, gs = to_south(ps), to_north(pn)
    ge, gw = to_west(pw), to_east(pe)
    r0, s0, dep_x, rows_n, rows_s, pay = call(
        residual_kernel, [plane, plane, wide, (8, L), (8, L), (NDEV, H)]
    )(fe, fn, wet, x0, depth, pe, pw, pn, ps, ge, gw, gn, gs)
    sn, ss = to_south(rows_s), to_north(rows_n)
    got = gather(pay)
    w0, s_x, faces, pay = call(first_kernel, [G, wide, (6,) + wide, (NDEV, H)])(got, coarse, r0, s0, dep_x, sn, ss)
    got = gather(pay)
    r1, s1, as1, x1, d0, ad0, w1, u0, net, num, pay = call(
        step_kernel, [plane] * 6 + [G, G, (3,) + G, (8, H), (NDEV, H)]
    )(got, coarse, w0, r0, s_x, faces, x0)
    got = gather(pay)
    return tuple(
        call(last_kernel, [plane, plane], out=lambda s: jax.ShapeDtypeStruct(s, f32))(
            got, w1, u0, net, num, coarse, r1, s1, as1, ad0, d0, x1, faces
        )
    )


def solution(mesh):
    return jax.shard_map(
        body,
        mesh=mesh,
        in_specs=(
            P(None, "lat", "lon"),
            P(None, "lat", "lon"),
            P(None, "lat", "lon"),
            P(),
            P("lat", "lon"),
            P("lat", "lon"),
            P("lat", "lon"),
            P(("lat", "lon"), None),
        ),
        out_specs=(P("lat", "lon"), P("lat", "lon")),
        check_vma=False,
    )
```

```python
import jax
import jax.numpy as jnp
from jax import lax
from jax.experimental import pallas as pl
from jax.experimental.pallas import tpu as pltpu
from jax.sharding import PartitionSpec as P

K = 75
R = 16
L = 256
H = 128
NLON = 16
NLAT = 16
NDEV = 256
EPS = 0.25
f32 = jnp.float32
highest = lax.Precision.HIGHEST
BOTH = ("lat", "lon")


def iota(shape, dim):
    return lax.broadcasted_iota(jnp.int32, shape, dim)


def in_vmem(shape):
    return pltpu.VMEM(shape, f32)


def call(kernel, out_shapes, out=in_vmem, **kw):
    vm = pl.BlockSpec(memory_space=pltpu.VMEM)

    def run(*args):
        return pl.pallas_call(
            kernel,
            out_shape=[out(s) for s in out_shapes],
            in_specs=[vm] * len(args),
            out_specs=[vm] * len(out_shapes),
            **kw,
        )(*[pltpu.with_memory_space_constraint(a, pltpu.VMEM) for a in args])

    return run


RX = R + 16
LX = L + 2 * H
ROWS = slice(8, 8 + R)
COLS = slice(H, H + L)


def beyond(v, rows, cols):
    n, m = v.shape
    if rows:
        v = pltpu.roll(v, -rows % n, 0)
    if cols:
        v = pltpu.roll(v, -cols % m, 1)
    return v


def apply_faces(faces, v):
    return faces[4] * v - (
        faces[0] * beyond(v, 0, 1)
        + faces[1] * beyond(v, 0, -1)
        + faces[2] * beyond(v, 1, 0)
        + faces[3] * beyond(v, -1, 0)
    )


def tile_sums(fields):
    n = len(fields)
    pick = (iota((L, H), 0) // 64 == iota((L, H), 1) % 4).astype(f32)
    cols = jnp.dot(jnp.concatenate(fields, axis=0), pick, precision=highest, preferred_element_type=f32)
    keep = iota((R, H), 0) // 4 == (iota((R, H), 1) % 16) // 4
    return [
        jnp.sum(jnp.where(keep, cols[R * i : R * i + R], 0.0), axis=0, keepdims=True)
        for i in range(n)
    ]


def pack(rows, rho):
    block = iota((1, H), 1) // 16
    out = jnp.zeros((1, H), f32)
    for f, row in enumerate(rows):
        out = jnp.where(block == (f + rho) % 8, row, out)
    return out


def unpack(got, f):
    shape = (NDEV // 8, 8, H)
    keep = iota(shape, 2) // 16 == (iota(shape, 1) + f) % 8
    flat = jnp.sum(jnp.where(keep, got.reshape(shape), 0.0), axis=1)
    return pltpu.roll(flat, (H - 16 * f) % H, 1) if f else flat


def coarse_rows(c_ref, w):
    acc = jnp.zeros((R, H), f32)
    for r in range(NDEV // 8):
        acc = acc + c_ref[:, H * r : H * r + H] * w[r : r + 1, :]
    col = jnp.sum(acc, axis=1, keepdims=True)
    return jnp.sum(jnp.where(iota((R, H), 0) == iota((R, H), 1) % 16, col, 0.0), axis=0, keepdims=True)


G = (NDEV // 8, H)


def c_east(q):
    lane = iota(G, 1)
    near = pltpu.roll(q, H - 1, 1)
    far = pltpu.roll(q, H - 13, 1)
    swap = jnp.where(iota(G, 0) % 2 == 0, pltpu.roll(far, G[0] - 1, 0), pltpu.roll(far, 1, 0))
    far = jnp.where(lane // 16 == 7, swap, far)
    return jnp.where(lane % 4 == 3, far, near)


def c_west(q):
    lane = iota(G, 1)
    near = pltpu.roll(q, 1, 1)
    far = pltpu.roll(q, 13, 1)
    swap = jnp.where(iota(G, 0) % 2 == 0, pltpu.roll(far, G[0] - 1, 0), pltpu.roll(far, 1, 0))
    far = jnp.where(lane // 16 == 0, swap, far)
    return jnp.where(lane % 4 == 0, far, near)


def c_north(q):
    near = pltpu.roll(q, H - 4, 1)
    far = pltpu.roll(pltpu.roll(q, 12, 1), G[0] - 2, 0)
    return jnp.where((iota(G, 1) % 16) // 4 == 3, far, near)


def c_south(q):
    near = pltpu.roll(q, 4, 1)
    far = pltpu.roll(pltpu.roll(q, H - 12, 1), 2, 0)
    return jnp.where((iota(G, 1) % 16) // 4 == 0, far, near)


def coarse_operator(q, count, link_e, link_n):
    flux_e = link_e * (q - c_east(q))
    flux_n = link_n * (q - c_north(q))
    return EPS * count * q + (flux_e - c_west(flux_e)) + (flux_n - c_south(flux_n))


def total(v):
    return jnp.sum(jnp.sum(v, axis=0, keepdims=True), axis=1, keepdims=True)


def neighbour(la, lo, da, do):
    a = la + da
    there = jnp.logical_and(a >= 0, a < NLAT)
    a = jnp.clip(a, 0, NLAT - 1)
    return a * NLON + (lo + do + NLON) % NLON, there


def lane_column(row, f, o):
    lane = iota((R, H), 1)
    hit = (lane // 16 == (f + o) % 8) & (lane % 16 == iota((R, H), 0))
    return jnp.sum(jnp.where(hit, jnp.broadcast_to(row, (R, H)), 0.0), axis=1, keepdims=True)


def lane_value(row, f, o):
    hit = iota((1, H), 1) == 16 * ((f + o) % 8)
    return jnp.sum(jnp.where(hit, row, 0.0), axis=1, keepdims=True)


def column_lanes(v, c):
    return jnp.sum(
        jnp.where(iota((R, H), 0) == iota((R, H), 1) % 16, v[:, c : c + 1], 0.0), axis=0, keepdims=True
    )


def spread(got_ref, la, lo):
    row = iota((RX, H), 0)
    lane = iota((RX, H), 1)
    ty = jnp.where(row < 8, 3, jnp.where(row < 8 + R, (row - 8) // 4, 0))
    src = jnp.zeros((RX, H), f32)
    l2 = iota((H, LX), 0)
    c2 = iota((H, LX), 1)
    pick = jnp.zeros((H, LX), f32)
    for do in (-1, 0, 1):
        o = (lo + do + NLON) % NLON
        south, mine, north = [
            jnp.broadcast_to(got_ref[pl.ds(neighbour(la, lo, da, do)[0], 1), :], (RX, H)) for da in (-1, 0, 1)
        ]
        part = jnp.where(row < 8, south, jnp.where(row < 8 + R, mine, north))
        src = jnp.where((lane // 16 == o % 8) & ((lane % 16) // 4 == ty), part, src)
        if do == 0:
            to = (c2 >= H) & (c2 < H + L) & (l2 % 4 == (c2 - H) // 64)
        elif do < 0:
            to = (c2 < H) & (l2 % 4 == 3)
        else:
            to = (c2 >= H + L) & (l2 % 4 == 0)
        pick = jnp.where(to & (l2 // 16 == o % 8), 1.0, pick)
    return jnp.dot(src, pick, precision=highest, preferred_element_type=f32)


def prolong_row(q_row):
    keep = (iota((R, H), 1) < 16) & (iota((R, H), 1) // 4 == iota((R, H), 0) // 4)
    pick = (iota((H, L), 0) % 4 == iota((H, L), 1) // 64).astype(f32)
    return jnp.dot(
        jnp.where(keep, jnp.broadcast_to(q_row, (R, H)), 0.0), pick, precision=highest, preferred_element_type=f32
    )


BOUNDS = (0, 20, 45, K)
CHUNKS = len(BOUNDS) - 1
NEAR = 0
FAR = 80
M_FORCE, M_WET1, M_WET2, M_DEPTH1, M_DEPTH2, M_X = range(6)
LAT_MISC = 160
LAT_ROWS = 168
LON_MISC = 2 * K
LON_LANES = 2 * H
C1, C2 = 8.0 / 12.0, 1.0 / 12.0


def lon_pick(prof, m, col, stride=2):
    at = stride * m.astype(jnp.int32) - stride + col
    lane = iota(prof.shape, 1)
    return jnp.sum(jnp.where((lane == at) & (m > 0.0), prof, 0.0), axis=1, keepdims=True)


def lat_pick(prof, m):
    level = iota((FAR, L), 0).astype(f32) + 1.0
    return jnp.sum(jnp.where(level == m, prof, 0.0), axis=0, keepdims=True)


def levels_kernel(thick, levels, mask, eta, rho, te, tn,
                  prefix, fe_out, fn_out, wet_out, x_out, depth_out, pe, pw, pn, ps, lat_a, lat_b, lon_a, lon_b,
                  t_s, lev_v, mask_v, eta_v, rho_v, te_v, tn_v, run, lon3, lat3, sem):
    small = [
        pltpu.make_async_copy(a, b, sem.at[3 * CHUNKS + i])
        for i, (a, b) in enumerate(((thick, t_s), (levels, lev_v), (mask, mask_v), (eta, eta_v)))
    ]
    for c in small:
        c.start()
    big = []
    for i, (a, b) in enumerate(((rho, rho_v), (te, te_v), (tn, tn_v))):
        big.append([])
        for c in range(CHUNKS):
            part = pl.ds(BOUNDS[c], BOUNDS[c + 1] - BOUNDS[c])
            big[-1].append(pltpu.make_async_copy(a.at[part], b.at[part], sem.at[CHUNKS * i + c]))
            big[-1][-1].start()
    for c in small:
        c.wait()
    own = (lev_v[...] * mask_v[...]).astype(f32)
    wet_out[...] = own
    x_out[...] = mask_v[...].astype(f32) * eta_v[...]
    zero = jnp.zeros((8, H), f32)
    lane8 = iota((8, H), 1)
    blocks = [(a, b, slice(8 * a, 8 * a + 8), slice(H * b, H * b + H)) for a in range(2) for b in range(2)]
    for a, b, rs, ls in blocks:
        d = zero
        wet = wet_out[rs, ls]
        for k in range(K):
            d = d + jnp.where(wet > float(k), t_s[k], 0.0)
        depth_out[rs, ls] = d
    for c in range(CHUNKS):
        big[0][c].wait()
        for a, b, rs, ls in blocks:
            lon_out = pe if b else pw
            if c == 0:
                p = g = third = zero
                prof = [zero, zero]
            else:
                p, g = run[0, rs, ls], run[1, rs, ls]
                prof = [lon_out[rs, :H], lon_out[rs, H:]]
                third = lon3[b, rs]
            for k in range(BOUNDS[c], BOUNDS[c + 1]):
                t = t_s[k]
                p = p + t * rho_v[k, rs, ls]
                g = g + t * p
                prefix[k, rs, ls] = g
                h, at = (2 * k) // H, (2 * k) % H
                moved = pltpu.roll(g, (at + 2) % H if b else at, 1) if (at + 2 * b) % H else g
                prof[h] = jnp.where((lane8 == at) | (lane8 == at + 1), moved, prof[h])
                shift = (k - (H - 3 if b else 2)) % H
                third = jnp.where(lane8 == k, pltpu.roll(g, shift, 1) if shift else g, third)
                lat_out = pn if a else ps
                near, far, past = (7, 6, 5) if a else (0, 1, 2)
                lat_out[NEAR + k : NEAR + k + 1, ls] = g[near : near + 1]
                lat_out[FAR + k : FAR + k + 1, ls] = g[far : far + 1]
                lat3[a, k : k + 1, ls] = g[past : past + 1]
            if c + 1 < CHUNKS:
                run[0, rs, ls] = p
                run[1, rs, ls] = g
            lon_out[rs, :H] = prof[0]
            lon_out[rs, H:] = prof[1]
            lon3[b, rs] = third
    for copies, tend, out in ((big[1], te_v, fe_out), (big[2], tn_v, fn_out)):
        for c in range(CHUNKS):
            copies[c].wait()
            for a, b, rs, ls in blocks:
                f = out[rs, ls] if c else zero
                wet = wet_out[rs, ls]
                for k in range(BOUNDS[c], BOUNDS[c + 1]):
                    f = f + jnp.where(wet > float(k), t_s[k], 0.0) * tend[k, rs, ls]
                out[rs, ls] = f
    fe, fn, d, x = fe_out[...], fn_out[...], depth_out[...], x_out[...]
    lane_t = iota((R, H), 1)

    def column(v, c):
        return v[:, c : c + 1]

    def line(v, r):
        return v[r : r + 1]

    for out, b, far_at, sign, c0, c1, c2 in ((pe, 1, 0, 1.0, L - 1, L - 2, L - 3), (pw, 0, 1, -1.0, 0, 1, 2)):
        o = column(own, c0)
        near = lon_pick(out[...], jnp.minimum(o, column(own, c1)), far_at)
        past = lon_pick(lon3[b], jnp.minimum(o, column(own, c2)), 0, 1)
        force = column(fe, c0) + sign * (C1 * near - C2 * past)
        tile = out[:, H:]
        for i, v in enumerate((force, o, column(own, c1), column(d, c0), column(d, c1), column(x, c0))):
            tile = jnp.where(lane_t == LON_MISC - H + i, v, tile)
        out[:, H:] = tile
    for out, a, sign, r0, r1, r2 in ((pn, 1, 1.0, R - 1, R - 2, R - 3), (ps, 0, -1.0, 0, 1, 2)):
        o = line(own, r0)
        near = lat_pick(out[FAR : 2 * FAR], jnp.minimum(o, line(own, r1)))
        past = lat_pick(lat3[a], jnp.minimum(o, line(own, r2)))
        force = line(fn, r0) + sign * (C1 * near - C2 * past)
        for i, v in enumerate((force, o, line(own, r1), line(d, r0), line(d, r1), line(x, r0))):
            out[LAT_MISC + i : LAT_MISC + i + 1] = v
    even = lax.axis_index("lat") % 2 == 0
    n, s = pn[...], ps[...]
    lat_a[...] = jnp.where(even, n, s)
    lat_b[...] = jnp.where(even, s, n)
    even = lax.axis_index("lon") % 2 == 0
    e, w = pe[...], pw[...]
    lon_a[...] = jnp.where(even, e, w)
    lon_b[...] = jnp.where(even, w, e)


def inner_kernel(prefix, wet, te, tn, fe_out, fn_out, m8, a8):
    own = wet[...]
    lane = iota((R, L), 1)
    row = iota((R, L), 0)
    for d, n in enumerate((1, 2)):
        m8[d] = jnp.where(lane < L - n, jnp.minimum(own, beyond(own, 0, n)), 0.0)
        m8[2 + d] = jnp.where(lane >= n, jnp.minimum(own, beyond(own, 0, -n)), 0.0)
        m8[4 + d] = jnp.where(row < R - n, jnp.minimum(own, beyond(own, n, 0)), 0.0)
        m8[6 + d] = jnp.where(row >= n, jnp.minimum(own, beyond(own, -n, 0)), 0.0)
    for a in range(2):
        for b in range(2):
            rs, ls = slice(8 * a, 8 * a + 8), slice(H * b, H * b + H)
            m = [m8[i, rs, ls] for i in range(8)]
            acc = [jnp.zeros((8, H), f32)] * 8
            for k in range(K):
                g = prefix[k, rs, ls]
                acc = [jnp.where(mi > float(k), g, ai) for mi, ai in zip(m, acc)]
            for i in range(8):
                a8[i, rs, ls] = acc[i]
    fe_out[...] = te[...] + C1 * (beyond(a8[0], 0, -1) - beyond(a8[2], 0, 1)) - C2 * (
        beyond(a8[1], 0, -2) - beyond(a8[3], 0, 2)
    )
    fn_out[...] = tn[...] + C1 * (beyond(a8[4], -1, 0) - beyond(a8[6], 1, 0)) - C2 * (
        beyond(a8[5], -2, 0) - beyond(a8[7], 2, 0)
    )


def residual_kernel(fe_in, fn_in, wet, x0, depth, pe, pw, pn, ps, lat_a, lat_b, lon_a, lon_b,
                    res, scaled, dep_x, rows_a, rows_b, pay, ge, gw, gn, gs):
    own = wet[...]
    la, lo = lax.axis_index("lat"), lax.axis_index("lon")
    lat_even, lon_even = la % 2 == 0, lo % 2 == 0
    a, b = lat_a[...], lat_b[...]
    gn[...] = jnp.where(lat_even, a, b)
    gs[...] = jnp.where(lat_even, b, a)
    a, b = lon_a[...], lon_b[...]
    ge[...] = jnp.where(lon_even, a, b)
    gw[...] = jnp.where(lon_even, b, a)
    lane = iota((R, L), 1)
    row = iota((R, L), 0)

    def lon_misc(ref, i):
        return ref[:, LON_MISC + i : LON_MISC + i + 1]

    def lat_misc(ref, i):
        there = la < NLAT - 1 if ref is gn else la > 0
        return jnp.where(there, ref[LAT_MISC + i : LAT_MISC + i + 1], 0.0)

    def from_lon(ref, m, col):
        return lon_pick(ref[...], m, col)

    def from_lat(ref, m, col):
        return lat_pick(ref[FAR : 2 * FAR] if col else ref[NEAR : NEAR + FAR], m)

    def cross(pick, got, sent, o1, o2, n1, n2, got_near, sent_near):
        gn_, sn_ = (0, 1) if got_near == 0 else (1, 0), (0, 1) if sent_near == 0 else (1, 0)
        first = (-8.0 * pick(got, jnp.minimum(o1, n1), gn_[0]) + pick(got, jnp.minimum(o1, n2), gn_[1])) / 12.0
        second = pick(got, jnp.minimum(o2, n1), gn_[0]) / 12.0
        theirs = (8.0 * pick(sent, jnp.minimum(n1, o1), sn_[0]) - pick(sent, jnp.minimum(n1, o2), sn_[1])) / 12.0
        return first, second, theirs

    fe = fe_in[...]
    fn = fn_in[...]
    a, b, far_e = cross(from_lon, ge, pe, own[:, L - 1 :], own[:, L - 2 : L - 1],
                        lon_misc(ge, M_WET1), lon_misc(ge, M_WET2), 0, 1)
    fe = fe + jnp.where(lane == L - 1, a, 0.0) + jnp.where(lane == L - 2, b, 0.0)
    fe_e = lon_misc(ge, M_FORCE) + far_e
    a, b, far_w = cross(from_lon, gw, pw, own[:, :1], own[:, 1:2],
                        lon_misc(gw, M_WET1), lon_misc(gw, M_WET2), 1, 0)
    fe = fe - jnp.where(lane == 0, a, 0.0) - jnp.where(lane == 1, b, 0.0)
    fe_w = lon_misc(gw, M_FORCE) - far_w
    a, b, far_n = cross(from_lat, gn, pn, own[R - 1 :], own[R - 2 : R - 1],
                        lat_misc(gn, M_WET1), lat_misc(gn, M_WET2), 0, 0)
    fn = fn + jnp.where(row == R - 1, a, 0.0) + jnp.where(row == R - 2, b, 0.0)
    fn_n = lat_misc(gn, M_FORCE) + far_n
    a, b, far_s = cross(from_lat, gs, ps, own[:1], own[1:2],
                        lat_misc(gs, M_WET1), lat_misc(gs, M_WET2), 0, 0)
    fn = fn - jnp.where(row == 0, a, 0.0) - jnp.where(row == 1, b, 0.0)
    fn_s = lat_misc(gs, M_FORCE) - far_s

    def shifts(v, e, w, n, s):
        return (
            jnp.where(lane == L - 1, e, beyond(v, 0, 1)),
            jnp.where(lane == 0, w, beyond(v, 0, -1)),
            jnp.where(row == R - 1, n, beyond(v, 1, 0)),
            jnp.where(row == 0, s, beyond(v, -1, 0)),
        )

    mask = (own > 0.0).astype(f32)
    d = depth[...]
    x = x0[...]
    face = [
        jnp.minimum(d, v)
        for v in shifts(d, lon_misc(ge, M_DEPTH1), lon_misc(gw, M_DEPTH1), lat_misc(gn, M_DEPTH1), lat_misc(gs, M_DEPTH1))
    ]
    diag = mask * (EPS + face[0] + face[1] + face[2] + face[3]) + (1.0 - mask)
    ax = diag * x
    for f, v in zip(face, shifts(x, lon_misc(ge, M_X), lon_misc(gw, M_X), lat_misc(gn, M_X), lat_misc(gs, M_X))):
        ax = ax - f * v
    f_e, f_w, _, _ = shifts(fe, fe_e, fe_w, fn_n, fn_s)
    _, _, f_n, f_s = shifts(fn, fe_e, fe_w, fn_n, fn_s)
    r = mask * 0.5 * (f_w - f_e + f_s - f_n) - ax
    s = r / diag
    res[...] = r
    scaled[...] = s
    rows_a[...] = jnp.where(lat_even, s[8:], s[:8])
    rows_b[...] = jnp.where(lat_even, s[:8], s[8:])
    dep_x[...] = jnp.zeros((RX, LX), f32)
    dep_x[ROWS, COLS] = d
    dep_x[7:8, COLS] = lat_misc(gs, M_DEPTH1)
    dep_x[6:7, COLS] = lat_misc(gs, M_DEPTH2)
    dep_x[8 + R : 9 + R, COLS] = lat_misc(gn, M_DEPTH1)
    dep_x[9 + R : 10 + R, COLS] = lat_misc(gn, M_DEPTH2)
    lane_t = iota((R, H), 1)
    dep_x[ROWS, :H] = jnp.where(
        lane_t == H - 1, lon_misc(gw, M_DEPTH1), jnp.where(lane_t == H - 2, lon_misc(gw, M_DEPTH2), 0.0)
    )
    dep_x[ROWS, H + L :] = jnp.where(
        lane_t == 0, lon_misc(ge, M_DEPTH1), jnp.where(lane_t == 1, lon_misc(ge, M_DEPTH2), 0.0)
    )
    rho = lo % 8
    (w,) = tile_sums([r * mask])
    pay[...] = jnp.broadcast_to(pack([w], rho), (NDEV, H))
    for do, c1, c2 in ((1, L - 1, L - 2), (-1, 0, 1)):
        at, _ = neighbour(la, lo, 0, do)
        pay[pl.ds(at, 1), :] = pack([w, column_lanes(s, c1), column_lanes(s, c2)], rho)
        for da, j in ((1, R - 1), (-1, 0)):
            at, there = neighbour(la, lo, da, do)
            at = jnp.where(there, at, la * NLON + lo)
            pay[pl.ds(at, 1), :] = pack(
                [w, jnp.broadcast_to(s[j : j + 1, c1 : c1 + 1], (1, H)), jnp.broadcast_to(d[j : j + 1, c1 : c1 + 1], (1, H))],
                rho,
            )


def first_kernel(got, coarse, res, scaled, dep_in, rows_a, rows_b, w_out, s_x, faces, pay):
    la, lo = lax.axis_index("lat"), lax.axis_index("lon")
    even = la % 2 == 0
    a, b = rows_a[...], rows_b[...]
    sn, ss = jnp.where(even, a, b), jnp.where(even, b, a)
    w = unpack(got[...], 0)
    w_out[...] = w
    q = coarse_rows(coarse, w)
    s = scaled[...]
    s_x[ROWS, COLS] = s
    s_x[:8, COLS] = jnp.where(la > 0, ss, 0.0)
    s_x[8 + R :, COLS] = jnp.where(la < NLAT - 1, sn, 0.0)
    lane = iota((R, H), 1)
    dep = dep_in[...]
    dep_x = faces.at[4]
    dep_x[...] = dep
    for do, cols, l1, l2 in ((1, slice(H + L, LX), 0, 1), (-1, slice(0, H), H - 1, H - 2)):
        at, _ = neighbour(la, lo, 0, do)
        o = (lo + do + NLON) % NLON
        msg = got[pl.ds(at, 1), :]
        s_x[ROWS, cols] = jnp.where(lane == l1, lane_column(msg, 1, o), jnp.where(lane == l2, lane_column(msg, 2, o), 0.0))
        for da, rows, j in ((1, slice(8 + R, RX), 0), (-1, slice(0, 8), 7)):
            at, there = neighbour(la, lo, da, do)
            msg = got[pl.ds(at, 1), :]
            here = (iota((8, H), 0) == j) & (iota((8, H), 1) == l1) & there
            s_x[rows, cols] = jnp.where(here, lane_value(msg, 1, o), 0.0)
            dep_x[rows, cols] = jnp.where(here, lane_value(msg, 2, o), 0.0)
    d = dep_x[...]
    mask = (d > 0.0).astype(f32)
    face = [jnp.minimum(d, beyond(d, a, b)) for a, b in ((0, 1), (0, -1), (1, 0), (-1, 0))]
    for i in range(4):
        faces[i] = face[i]
    diag = mask * (EPS + face[0] + face[1] + face[2] + face[3]) + (1.0 - mask)
    faces[4] = diag
    faces[5] = mask
    own = (ROWS, COLS)
    a_s = apply_faces(face + [diag], s_x[...])[own]
    sums = tile_sums([
        a_s * mask[own],
        mask[own],
        jnp.where(iota((R, L), 1) % 64 == 63, face[0][own], 0.0),
        jnp.where(iota((R, L), 0) % 4 == 3, face[2][own], 0.0),
        s * a_s,
        res[...] * s,
    ])
    pay[...] = jnp.broadcast_to(pack([q] + sums, lo % 8), (NDEV, H))


def step_kernel(got, coarse, w_in, res, s_x, faces, x0,
                r_out, s_out, as_out, x_out, d_out, ad_out, w_out, u_out, net_out, num_out, pay):
    la, lo = lax.axis_index("lat"), lax.axis_index("lon")
    own = (ROWS, COLS)
    g = got[...]
    q, a, count, link_e, link_n, cc, ee = [unpack(g, f) for f in range(7)]
    w = w_in[...]
    tq = coarse_operator(q, count, link_e, link_n)
    u = a + tq
    d_a_d = total(cc + q * (2.0 * a + tq))
    rz = total(ee + w * q)
    alpha = rz / d_a_d
    w = w - alpha * u
    w_out[...] = w
    u_out[...] = u
    net_out[0] = count
    net_out[1] = link_e
    net_out[2] = link_n
    num_out[0:1] = jnp.broadcast_to(rz, (1, H))
    num_out[1:2] = jnp.broadcast_to(d_a_d, (1, H))
    num_out[2:] = jnp.zeros((6, H), f32)
    q = coarse_rows(coarse, w)
    face = [faces[i] for i in range(6)]
    mask = face[5]
    s = s_x[...]
    d = s + mask * spread(got, la, lo)
    ad = apply_faces(face, d)
    s = s - alpha * (ad / face[4])
    a_s = apply_faces(face, s)[own]
    ad = ad[own]
    s = s[own]
    r = res[...] - alpha * ad
    r_out[...] = r
    s_out[...] = s
    as_out[...] = a_s
    x_out[...] = x0[...] + alpha * d[own]
    d_out[...] = d[own]
    ad_out[...] = ad
    sums = tile_sums([a_s * mask[own], s * a_s, r * s, s * ad])
    pay[...] = jnp.broadcast_to(pack([q] + sums, lo % 8), (NDEV, H))


def last_kernel(got, w_in, u_in, net, num, coarse, res, scaled, a_s, ad, d_in, x_in, faces, surface, precond):
    la, lo = lax.axis_index("lat"), lax.axis_index("lon")
    own = (ROWS, COLS)
    g = got[...]
    q, a, cc, ee, hh = [unpack(g, f) for f in range(5)]
    w = w_in[...]
    u0 = u_in[...]
    rz0 = num[0:1, :1]
    dad0 = num[1:2, :1]
    tq = coarse_operator(q, net[0], net[1], net[2])
    zaz = total(cc + q * (2.0 * a + tq))
    rz = total(ee + w * q)
    zad = total(hh + q * u0)
    beta = rz / rz0
    alpha = rz / (zaz + 2.0 * beta * zad + beta * beta * dad0)
    q2 = prolong_row(coarse_rows(coarse, w - alpha * (a + tq + beta * u0)))
    face = [faces[i] for i in range(6)]
    mask = face[5]
    pq = mask * spread(got, la, lo)
    d = scaled[...] + pq[own] + beta * d_in[...]
    ad1 = a_s[...] + apply_faces(face, pq)[own] + beta * ad[...]
    surface[...] = x_in[...] + alpha * d
    precond[...] = (res[...] - alpha * ad1) / face[4][own] + q2 * mask[own]


def swap_a(v, axis):
    return lax.ppermute(v, axis, [(i, i ^ 1) for i in range(16)])


def swap_b(v, axis):
    return lax.ppermute(v, axis, [(i, (i + 1 if i % 2 else i - 1) % 16) for i in range(16)])


def gather(pay):
    return lax.all_to_all(pay, BOTH, 0, 0, tiled=True)


def body(density, tend_east, tend_north, thickness, levels, ocean_mask, eta_prev, coarse):
    plane, wide = (R, L), (RX, LX)
    lon_msg, lat_msg = (R, LON_LANES), (LAT_ROWS, L)
    vm = pl.BlockSpec(memory_space=pltpu.VMEM)
    prefix, te, tn, wet, x0, depth, pe, pw, pn, ps, lat_a, lat_b, lon_a, lon_b = pl.pallas_call(
        levels_kernel,
        in_specs=[pl.BlockSpec(memory_space=pl.ANY)] * 7,
        out_specs=[vm] * 14,
        out_shape=[in_vmem(s) for s in [(K, R, L)] + [plane] * 5 + ([lon_msg] * 2 + [lat_msg] * 2) + ([lat_msg] * 2 + [lon_msg] * 2)],
        scratch_shapes=[
            pltpu.SMEM((K,), f32),
            pltpu.VMEM(plane, jnp.int32),
            pltpu.VMEM(plane, jnp.int32),
            pltpu.VMEM(plane, f32),
            pltpu.VMEM((K, R, L), f32),
            pltpu.VMEM((K, R, L), f32),
            pltpu.VMEM((K, R, L), f32),
            pltpu.VMEM((2, R, L), f32),
            pltpu.VMEM((2, R, H), f32),
            pltpu.VMEM((2, FAR, L), f32),
            pltpu.SemaphoreType.DMA((3 * CHUNKS + 4,)),
        ],
        name="levels",
    )(thickness, levels, ocean_mask, eta_prev, density, tend_east, tend_north)
    lat_a, lat_b = swap_a(lat_a, "lat"), swap_b(lat_b, "lat")
    lon_a, lon_b = swap_a(lon_a, "lon"), swap_b(lon_b, "lon")
    fe, fn = call(
        inner_kernel, [plane, plane], scratch_shapes=[pltpu.VMEM((8, R, L), f32), pltpu.VMEM((8, R, L), f32)]
    )(prefix, wet, te, tn)
    r0, s0, dep_x, rows_a, rows_b, pay = call(
        residual_kernel,
        [plane, plane, wide, (8, L), (8, L), (NDEV, H)],
        scratch_shapes=[pltpu.VMEM(x, f32) for x in (lon_msg, lon_msg, lat_msg, lat_msg)],
    )(fe, fn, wet, x0, depth, pe, pw, pn, ps, lat_a, lat_b, lon_a, lon_b)
    rows_a, rows_b = swap_a(rows_a, "lat"), swap_b(rows_b, "lat")
    got = gather(pay)
    w0, s_x, faces, pay = call(first_kernel, [G, wide, (6,) + wide, (NDEV, H)])(
        got, coarse, r0, s0, dep_x, rows_a, rows_b
    )
    got = gather(pay)
    r1, s1, as1, x1, d0, ad0, w1, u0, net, num, pay = call(
        step_kernel, [plane] * 6 + [G, G, (3,) + G, (8, H), (NDEV, H)]
    )(got, coarse, w0, r0, s_x, faces, x0)
    got = gather(pay)
    return tuple(
        call(last_kernel, [plane, plane], out=lambda s: jax.ShapeDtypeStruct(s, f32))(
            got, w1, u0, net, num, coarse, r1, s1, as1, ad0, d0, x1, faces
        )
    )


def solution(mesh):
    return jax.shard_map(
        body,
        mesh=mesh,
        in_specs=(
            P(None, "lat", "lon"),
            P(None, "lat", "lon"),
            P(None, "lat", "lon"),
            P(),
            P("lat", "lon"),
            P("lat", "lon"),
            P("lat", "lon"),
            P(("lat", "lon"), None),
        ),
        out_specs=(P("lat", "lon"), P("lat", "lon")),
        check_vma=False,
    )
```

```python
import jax
import jax.numpy as jnp
from jax import lax
from jax.experimental import pallas as pl
from jax.experimental.pallas import tpu as pltpu
from jax.sharding import PartitionSpec as P

K = 75
R = 16
L = 256
H = 128
NLON = 16
NLAT = 16
NDEV = 256
EPS = 0.25
f32 = jnp.float32
highest = lax.Precision.HIGHEST
BOTH = ("lat", "lon")


def iota(shape, dim):
    return lax.broadcasted_iota(jnp.int32, shape, dim)


def in_vmem(shape):
    return pltpu.VMEM(shape, f32)


def call(kernel, out_shapes, name, out=in_vmem, **kw):
    vm = pl.BlockSpec(memory_space=pltpu.VMEM)

    def run(*args):
        return pl.pallas_call(
            kernel,
            out_shape=[out(s) for s in out_shapes],
            in_specs=[vm] * len(args),
            out_specs=[vm] * len(out_shapes),
            name=name,
            **kw,
        )(*[pltpu.with_memory_space_constraint(a, pltpu.VMEM) for a in args])

    return run


RX = R + 16
LX = L + 2 * H
ROWS = slice(8, 8 + R)
COLS = slice(H, H + L)


def beyond(v, rows, cols):
    n, m = v.shape
    if rows:
        v = pltpu.roll(v, -rows % n, 0)
    if cols:
        v = pltpu.roll(v, -cols % m, 1)
    return v


def apply_faces(faces, v):
    return faces[4] * v - (
        faces[0] * beyond(v, 0, 1)
        + faces[1] * beyond(v, 0, -1)
        + faces[2] * beyond(v, 1, 0)
        + faces[3] * beyond(v, -1, 0)
    )


def tile_sums(fields):
    n = len(fields)
    pick = (iota((L, H), 0) // 64 == iota((L, H), 1) % 4).astype(f32)
    cols = jnp.dot(jnp.concatenate(fields, axis=0), pick, precision=highest, preferred_element_type=f32)
    keep = iota((R, H), 0) // 4 == (iota((R, H), 1) % 16) // 4
    return [
        jnp.sum(jnp.where(keep, cols[R * i : R * i + R], 0.0), axis=0, keepdims=True)
        for i in range(n)
    ]


def pack(rows, rho):
    block = iota((1, H), 1) // 16
    out = jnp.zeros((1, H), f32)
    for f, row in enumerate(rows):
        out = jnp.where(block == (f + rho) % 8, row, out)
    return out


def unpack(got, f):
    shape = (NDEV // 8, 8, H)
    keep = iota(shape, 2) // 16 == (iota(shape, 1) + f) % 8
    flat = jnp.sum(jnp.where(keep, got.reshape(shape), 0.0), axis=1)
    return pltpu.roll(flat, (H - 16 * f) % H, 1) if f else flat


def coarse_rows(c_ref, w):
    acc = jnp.zeros((R, H), f32)
    for r in range(NDEV // 8):
        acc = acc + c_ref[:, H * r : H * r + H] * w[r : r + 1, :]
    col = jnp.sum(acc, axis=1, keepdims=True)
    return jnp.sum(jnp.where(iota((R, H), 0) == iota((R, H), 1) % 16, col, 0.0), axis=0, keepdims=True)


G = (NDEV // 8, H)


def c_east(q):
    lane = iota(G, 1)
    near = pltpu.roll(q, H - 1, 1)
    far = pltpu.roll(q, H - 13, 1)
    swap = jnp.where(iota(G, 0) % 2 == 0, pltpu.roll(far, G[0] - 1, 0), pltpu.roll(far, 1, 0))
    far = jnp.where(lane // 16 == 7, swap, far)
    return jnp.where(lane % 4 == 3, far, near)


def c_west(q):
    lane = iota(G, 1)
    near = pltpu.roll(q, 1, 1)
    far = pltpu.roll(q, 13, 1)
    swap = jnp.where(iota(G, 0) % 2 == 0, pltpu.roll(far, G[0] - 1, 0), pltpu.roll(far, 1, 0))
    far = jnp.where(lane // 16 == 0, swap, far)
    return jnp.where(lane % 4 == 0, far, near)


def c_north(q):
    near = pltpu.roll(q, H - 4, 1)
    far = pltpu.roll(pltpu.roll(q, 12, 1), G[0] - 2, 0)
    return jnp.where((iota(G, 1) % 16) // 4 == 3, far, near)


def c_south(q):
    near = pltpu.roll(q, 4, 1)
    far = pltpu.roll(pltpu.roll(q, H - 12, 1), 2, 0)
    return jnp.where((iota(G, 1) % 16) // 4 == 0, far, near)


def coarse_operator(q, count, link_e, link_n):
    flux_e = link_e * (q - c_east(q))
    flux_n = link_n * (q - c_north(q))
    return EPS * count * q + (flux_e - c_west(flux_e)) + (flux_n - c_south(flux_n))


def total(v):
    return jnp.sum(jnp.sum(v, axis=0, keepdims=True), axis=1, keepdims=True)


def neighbour(la, lo, da, do):
    a = la + da
    there = jnp.logical_and(a >= 0, a < NLAT)
    a = jnp.clip(a, 0, NLAT - 1)
    return a * NLON + (lo + do + NLON) % NLON, there


def lane_column(row, f, o):
    lane = iota((R, H), 1)
    hit = (lane // 16 == (f + o) % 8) & (lane % 16 == iota((R, H), 0))
    return jnp.sum(jnp.where(hit, jnp.broadcast_to(row, (R, H)), 0.0), axis=1, keepdims=True)


def lane_value(row, f, o):
    hit = iota((1, H), 1) == 16 * ((f + o) % 8)
    return jnp.sum(jnp.where(hit, row, 0.0), axis=1, keepdims=True)


def column_lanes(v, c):
    return jnp.sum(
        jnp.where(iota((R, H), 0) == iota((R, H), 1) % 16, v[:, c : c + 1], 0.0), axis=0, keepdims=True
    )


def spread(got_ref, la, lo):
    row = iota((RX, H), 0)
    lane = iota((RX, H), 1)
    ty = jnp.where(row < 8, 3, jnp.where(row < 8 + R, (row - 8) // 4, 0))
    src = jnp.zeros((RX, H), f32)
    l2 = iota((H, LX), 0)
    c2 = iota((H, LX), 1)
    pick = jnp.zeros((H, LX), f32)
    for do in (-1, 0, 1):
        o = (lo + do + NLON) % NLON
        south, mine, north = [
            jnp.broadcast_to(got_ref[pl.ds(neighbour(la, lo, da, do)[0], 1), :], (RX, H)) for da in (-1, 0, 1)
        ]
        part = jnp.where(row < 8, south, jnp.where(row < 8 + R, mine, north))
        src = jnp.where((lane // 16 == o % 8) & ((lane % 16) // 4 == ty), part, src)
        if do == 0:
            to = (c2 >= H) & (c2 < H + L) & (l2 % 4 == (c2 - H) // 64)
        elif do < 0:
            to = (c2 < H) & (l2 % 4 == 3)
        else:
            to = (c2 >= H + L) & (l2 % 4 == 0)
        pick = jnp.where(to & (l2 // 16 == o % 8), 1.0, pick)
    return jnp.dot(src, pick, precision=highest, preferred_element_type=f32)


def prolong_rows(rows):
    keep = (iota((R, H), 1) < 16) & (iota((R, H), 1) // 4 == iota((R, H), 0) // 4)
    pick = (iota((H, L), 0) % 4 == iota((H, L), 1) // 64).astype(f32)
    src = jnp.concatenate([jnp.where(keep, jnp.broadcast_to(q, (R, H)), 0.0) for q in rows], axis=0)
    out = jnp.dot(src, pick, precision=highest, preferred_element_type=f32)
    return [out[R * i : R * i + R] for i in range(len(rows))]


BOUNDS = (0, 25, 60, K)
CHUNKS = len(BOUNDS) - 1
NEAR = 0
FAR = 80
M_FORCE, M_WET1, M_WET2, M_DEPTH1, M_DEPTH2, M_X = range(6)
LAT_MISC = 160
HALF = FAR * R
LAT_ROWS = 168
LON_MISC = 3 * K
LON_LANES = 2 * H
C1, C2 = 8.0 / 12.0, 1.0 / 12.0


def lon_pick(prof, m, col):
    at = 3 * m.astype(jnp.int32) - 3 + col
    lane = iota(prof.shape, 1)
    return jnp.sum(jnp.where((lane == at) & (m > 0.0), prof, 0.0), axis=1, keepdims=True)


def lat_pick(prof, m):
    level = iota((FAR, L), 0).astype(f32) + 1.0
    return jnp.sum(jnp.where(level == m, prof, 0.0), axis=0, keepdims=True)


def levels_kernel(thick, levels, mask, eta, rho, te, tn,
                  prefix, fe_out, fn_out, wet_out, x_out, depth_out, pe, pw, pn, ps, lat_a, lat_b, lon_a, lon_b,
                  t_s, lev_v, mask_v, eta_v, rho_v, te_v, tn_v, run, sem):
    small = [
        pltpu.make_async_copy(a, b, sem.at[3 * CHUNKS + i])
        for i, (a, b) in enumerate(((thick, t_s), (levels, lev_v), (mask, mask_v), (eta, eta_v)))
    ]
    for c in small:
        c.start()
    big = [[], [], []]
    arrays = ((rho, rho_v), (te, te_v), (tn, tn_v))
    for i, c in [(0, c) for c in range(CHUNKS)] + [(i, c) for c in range(CHUNKS) for i in (1, 2)]:
        part = pl.ds(BOUNDS[c], BOUNDS[c + 1] - BOUNDS[c])
        a, b = arrays[i]
        big[i].append(pltpu.make_async_copy(a.at[part], b.at[part], sem.at[CHUNKS * i + c]))
        big[i][-1].start()
    for c in small:
        c.wait()
    own = (lev_v[...] * mask_v[...]).astype(f32)
    wet_out[...] = own
    x_out[...] = mask_v[...].astype(f32) * eta_v[...]
    zero = jnp.zeros((8, H), f32)
    lane8 = iota((8, H), 1)
    blocks = [(a, b, slice(8 * a, 8 * a + 8), slice(H * b, H * b + H)) for a in range(2) for b in range(2)]
    for c in range(CHUNKS):
        big[0][c].wait()
        state = []
        for a, b, rs, ls in blocks:
            lon_out = pe if b else pw
            if c == 0:
                state.append([zero] * 4)
            else:
                state.append([run[0, rs, ls], run[1, rs, ls], lon_out[rs, :H], lon_out[rs, H:]])
        for k in range(BOUNDS[c], BOUNDS[c + 1]):
            t = t_s[k]
            at = 3 * k
            halves = [(h, (lane8 >= at - H * h) & (lane8 < at - H * h + 3)) for h in (0, 1) if at < H * h + H and at + 2 >= H * h]
            for (a, b, rs, ls), v in zip(blocks, state):
                v[0] = v[0] + t * rho_v[k, rs, ls]
                v[1] = g = v[1] + t * v[0]
                prefix[HALF * b + R * k + 8 * a : HALF * b + R * k + 8 * a + 8, :] = g
                shift = (at + 3 * b) % H
                moved = pltpu.roll(g, shift, 1) if shift else g
                for h, here in halves:
                    v[2 + h] = jnp.where(here, moved, v[2 + h])
        for (a, b, rs, ls), v in zip(blocks, state):
            lon_out = pe if b else pw
            run[0, rs, ls], run[1, rs, ls] = v[0], v[1]
            lon_out[rs, :H] = v[2]
            lon_out[rs, H:] = v[3]
    x = x_out[...]
    lane_t = iota((R, H), 1)

    def column(v, c):
        return v[:, c : c + 1]

    def line(v, r):
        return v[r : r + 1]

    def profile(r):
        return jnp.concatenate([prefix[pl.ds(HALF * b + r, FAR, stride=R), :] for b in range(2)], axis=1)

    added = []
    for out, past_at, c0, c1, c2 in ((pe, 0, L - 1, L - 2, L - 3), (pw, 2, 0, 1, 2)):
        o = column(own, c0)
        near = lon_pick(out[...], jnp.minimum(o, column(own, c1)), 1)
        past = lon_pick(out[...], jnp.minimum(o, column(own, c2)), past_at)
        added.append(C1 * near - C2 * past)
        tile = out[:, H:]
        for i, v in ((M_WET1, o), (M_WET2, column(own, c1)), (M_X, column(x, c0))):
            tile = jnp.where(lane_t == LON_MISC - H + i, v, tile)
        out[:, H:] = tile
    for out, r0, r1, r2 in ((pn, R - 1, R - 2, R - 3), (ps, 0, 1, 2)):
        out[NEAR : NEAR + FAR] = profile(r0)
        far = profile(r1)
        out[FAR : 2 * FAR] = far
        o = line(own, r0)
        near = lat_pick(far, jnp.minimum(o, line(own, r1)))
        past = lat_pick(profile(r2), jnp.minimum(o, line(own, r2)))
        added.append(C1 * near - C2 * past)
        for i, v in ((M_WET1, o), (M_WET2, line(own, r1)), (M_X, line(x, r0))):
            out[LAT_MISC + i : LAT_MISC + i + 1] = v
    lat_even = lax.axis_index("lat") % 2 == 0
    n, s = pn[...], ps[...]
    lat_a[...] = jnp.where(lat_even, n, s)
    lat_b[...] = jnp.where(lat_even, s, n)
    for c in range(CHUNKS):
        big[1][c].wait()
        big[2][c].wait()
        for a, b, rs, ls in blocks:
            d, fe, fn = [v[rs, ls] if c else zero for v in (depth_out, fe_out, fn_out)]
            wet = wet_out[rs, ls]
            for k in range(BOUNDS[c], BOUNDS[c + 1]):
                ta = jnp.where(wet > float(k), t_s[k], 0.0)
                d = d + ta
                fe = fe + ta * te_v[k, rs, ls]
                fn = fn + ta * tn_v[k, rs, ls]
            depth_out[rs, ls] = d
            fe_out[rs, ls] = fe
            fn_out[rs, ls] = fn
    d, fe, fn = depth_out[...], fe_out[...], fn_out[...]
    for out, add, c0, c1 in ((pe, added[0], L - 1, L - 2), (pw, -added[1], 0, 1)):
        tile = out[:, H:]
        for i, v in ((M_FORCE, column(fe, c0) + add), (M_DEPTH1, column(d, c0)), (M_DEPTH2, column(d, c1))):
            tile = jnp.where(lane_t == LON_MISC - H + i, v, tile)
        out[:, H:] = tile
    lon_even = lax.axis_index("lon") % 2 == 0
    e, w = pe[...], pw[...]
    lon_a[...] = jnp.where(lon_even, e, w)
    lon_b[...] = jnp.where(lon_even, w, e)
    for i, n, s in (
        (M_FORCE, line(fn, R - 1) + added[2], line(fn, 0) - added[3]),
        (M_DEPTH1, line(d, R - 1), line(d, 0)),
        (M_DEPTH2, line(d, R - 2), line(d, 1)),
    ):
        lat_a[LAT_MISC + i : LAT_MISC + i + 1] = jnp.where(lat_even, n, s)
        lat_b[LAT_MISC + i : LAT_MISC + i + 1] = jnp.where(lat_even, s, n)


def inner_kernel(prefix, wet, te, tn, fe_out, fn_out, m8, a8):
    own = wet[...]
    lane = iota((R, L), 1)
    row = iota((R, L), 0)
    for d, n in enumerate((1, 2)):
        m8[d] = jnp.where(lane < L - n, jnp.minimum(own, beyond(own, 0, n)), 0.0)
        m8[2 + d] = jnp.where(lane >= n, jnp.minimum(own, beyond(own, 0, -n)), 0.0)
        m8[4 + d] = jnp.where(row < R - n, jnp.minimum(own, beyond(own, n, 0)), 0.0)
        m8[6 + d] = jnp.where(row >= n, jnp.minimum(own, beyond(own, -n, 0)), 0.0)
    for a in range(2):
        for b in range(2):
            rs, ls = slice(8 * a, 8 * a + 8), slice(H * b, H * b + H)
            m = [m8[i, rs, ls] for i in range(8)]
            acc = [jnp.zeros((8, H), f32)] * 8
            for k in range(K):
                g = prefix[HALF * b + R * k + 8 * a : HALF * b + R * k + 8 * a + 8, :]
                acc = [jnp.where(mi > float(k), g, ai) for mi, ai in zip(m, acc)]
            for i in range(8):
                a8[i, rs, ls] = acc[i]
    fe_out[...] = te[...] + C1 * (beyond(a8[0], 0, -1) - beyond(a8[2], 0, 1)) - C2 * (
        beyond(a8[1], 0, -2) - beyond(a8[3], 0, 2)
    )
    fn_out[...] = tn[...] + C1 * (beyond(a8[4], -1, 0) - beyond(a8[6], 1, 0)) - C2 * (
        beyond(a8[5], -2, 0) - beyond(a8[7], 2, 0)
    )


def residual_kernel(fe_in, fn_in, wet, x0, depth, pe, pw, pn, ps, lat_a, lat_b, lon_a, lon_b,
                    res, scaled, dep_x, rows_a, rows_b, pay, ge, gw, gn, gs):
    own = wet[...]
    la, lo = lax.axis_index("lat"), lax.axis_index("lon")
    lat_even, lon_even = la % 2 == 0, lo % 2 == 0
    a, b = lat_a[...], lat_b[...]
    gn[...] = jnp.where(lat_even, a, b)
    gs[...] = jnp.where(lat_even, b, a)
    a, b = lon_a[...], lon_b[...]
    ge[...] = jnp.where(lon_even, a, b)
    gw[...] = jnp.where(lon_even, b, a)
    lane = iota((R, L), 1)
    row = iota((R, L), 0)

    def lon_misc(ref, i):
        return ref[:, LON_MISC + i : LON_MISC + i + 1]

    def lat_misc(ref, i):
        there = la < NLAT - 1 if ref is gn else la > 0
        return jnp.where(there, ref[LAT_MISC + i : LAT_MISC + i + 1], 0.0)

    def from_lon(ref, m, col):
        return lon_pick(ref[...], m, col)

    def from_lat(ref, m, col):
        return lat_pick(ref[FAR : 2 * FAR] if col else ref[NEAR : NEAR + FAR], m)

    def cross(pick, got, sent, o1, o2, n1, n2, got_near, sent_near):
        gn_, sn_ = (got_near, 1), (sent_near, 1)
        first = (-8.0 * pick(got, jnp.minimum(o1, n1), gn_[0]) + pick(got, jnp.minimum(o1, n2), gn_[1])) / 12.0
        second = pick(got, jnp.minimum(o2, n1), gn_[0]) / 12.0
        theirs = (8.0 * pick(sent, jnp.minimum(n1, o1), sn_[0]) - pick(sent, jnp.minimum(n1, o2), sn_[1])) / 12.0
        return first, second, theirs

    fe = fe_in[...]
    fn = fn_in[...]
    a, b, far_e = cross(from_lon, ge, pe, own[:, L - 1 :], own[:, L - 2 : L - 1],
                        lon_misc(ge, M_WET1), lon_misc(ge, M_WET2), 0, 2)
    fe = fe + jnp.where(lane == L - 1, a, 0.0) + jnp.where(lane == L - 2, b, 0.0)
    fe_e = lon_misc(ge, M_FORCE) + far_e
    a, b, far_w = cross(from_lon, gw, pw, own[:, :1], own[:, 1:2],
                        lon_misc(gw, M_WET1), lon_misc(gw, M_WET2), 2, 0)
    fe = fe - jnp.where(lane == 0, a, 0.0) - jnp.where(lane == 1, b, 0.0)
    fe_w = lon_misc(gw, M_FORCE) - far_w
    a, b, far_n = cross(from_lat, gn, pn, own[R - 1 :], own[R - 2 : R - 1],
                        lat_misc(gn, M_WET1), lat_misc(gn, M_WET2), 0, 0)
    fn = fn + jnp.where(row == R - 1, a, 0.0) + jnp.where(row == R - 2, b, 0.0)
    fn_n = lat_misc(gn, M_FORCE) + far_n
    a, b, far_s = cross(from_lat, gs, ps, own[:1], own[1:2],
                        lat_misc(gs, M_WET1), lat_misc(gs, M_WET2), 0, 0)
    fn = fn - jnp.where(row == 0, a, 0.0) - jnp.where(row == 1, b, 0.0)
    fn_s = lat_misc(gs, M_FORCE) - far_s

    def shifts(v, e, w, n, s):
        return (
            jnp.where(lane == L - 1, e, beyond(v, 0, 1)),
            jnp.where(lane == 0, w, beyond(v, 0, -1)),
            jnp.where(row == R - 1, n, beyond(v, 1, 0)),
            jnp.where(row == 0, s, beyond(v, -1, 0)),
        )

    mask = (own > 0.0).astype(f32)
    d = depth[...]
    x = x0[...]
    face = [
        jnp.minimum(d, v)
        for v in shifts(d, lon_misc(ge, M_DEPTH1), lon_misc(gw, M_DEPTH1), lat_misc(gn, M_DEPTH1), lat_misc(gs, M_DEPTH1))
    ]
    diag = mask * (EPS + face[0] + face[1] + face[2] + face[3]) + (1.0 - mask)
    ax = diag * x
    for f, v in zip(face, shifts(x, lon_misc(ge, M_X), lon_misc(gw, M_X), lat_misc(gn, M_X), lat_misc(gs, M_X))):
        ax = ax - f * v
    f_e, f_w, _, _ = shifts(fe, fe_e, fe_w, fn_n, fn_s)
    _, _, f_n, f_s = shifts(fn, fe_e, fe_w, fn_n, fn_s)
    r = mask * 0.5 * (f_w - f_e + f_s - f_n) - ax
    s = r / diag
    res[...] = r
    scaled[...] = s
    rows_a[...] = jnp.where(lat_even, s[8:], s[:8])
    rows_b[...] = jnp.where(lat_even, s[:8], s[8:])
    dep_x[...] = jnp.zeros((RX, LX), f32)
    dep_x[ROWS, COLS] = d
    dep_x[7:8, COLS] = lat_misc(gs, M_DEPTH1)
    dep_x[6:7, COLS] = lat_misc(gs, M_DEPTH2)
    dep_x[8 + R : 9 + R, COLS] = lat_misc(gn, M_DEPTH1)
    dep_x[9 + R : 10 + R, COLS] = lat_misc(gn, M_DEPTH2)
    lane_t = iota((R, H), 1)
    dep_x[ROWS, :H] = jnp.where(
        lane_t == H - 1, lon_misc(gw, M_DEPTH1), jnp.where(lane_t == H - 2, lon_misc(gw, M_DEPTH2), 0.0)
    )
    dep_x[ROWS, H + L :] = jnp.where(
        lane_t == 0, lon_misc(ge, M_DEPTH1), jnp.where(lane_t == 1, lon_misc(ge, M_DEPTH2), 0.0)
    )
    rho = lo % 8
    (w,) = tile_sums([r * mask])
    pay[...] = jnp.broadcast_to(pack([w], rho), (NDEV, H))
    for do, c1, c2 in ((1, L - 1, L - 2), (-1, 0, 1)):
        at, _ = neighbour(la, lo, 0, do)
        pay[pl.ds(at, 1), :] = pack([w, column_lanes(s, c1), column_lanes(s, c2)], rho)
        for da, j in ((1, R - 1), (-1, 0)):
            at, there = neighbour(la, lo, da, do)
            at = jnp.where(there, at, la * NLON + lo)
            pay[pl.ds(at, 1), :] = pack(
                [w, jnp.broadcast_to(s[j : j + 1, c1 : c1 + 1], (1, H)), jnp.broadcast_to(d[j : j + 1, c1 : c1 + 1], (1, H))],
                rho,
            )


def first_kernel(got, coarse, res, scaled, dep_in, rows_a, rows_b, w_out, q_out, s_x, faces, pay):
    la, lo = lax.axis_index("lat"), lax.axis_index("lon")
    even = la % 2 == 0
    a, b = rows_a[...], rows_b[...]
    sn, ss = jnp.where(even, a, b), jnp.where(even, b, a)
    w = unpack(got[...], 0)
    w_out[...] = w
    q = coarse_rows(coarse, w)
    q_out[...] = jnp.broadcast_to(q, (8, H))
    s = scaled[...]
    s_x[ROWS, COLS] = s
    s_x[:8, COLS] = jnp.where(la > 0, ss, 0.0)
    s_x[8 + R :, COLS] = jnp.where(la < NLAT - 1, sn, 0.0)
    lane = iota((R, H), 1)
    dep = dep_in[...]
    dep_x = faces.at[4]
    dep_x[...] = dep
    for do, cols, l1, l2 in ((1, slice(H + L, LX), 0, 1), (-1, slice(0, H), H - 1, H - 2)):
        at, _ = neighbour(la, lo, 0, do)
        o = (lo + do + NLON) % NLON
        msg = got[pl.ds(at, 1), :]
        s_x[ROWS, cols] = jnp.where(lane == l1, lane_column(msg, 1, o), jnp.where(lane == l2, lane_column(msg, 2, o), 0.0))
        for da, rows, j in ((1, slice(8 + R, RX), 0), (-1, slice(0, 8), 7)):
            at, there = neighbour(la, lo, da, do)
            msg = got[pl.ds(at, 1), :]
            here = (iota((8, H), 0) == j) & (iota((8, H), 1) == l1) & there
            s_x[rows, cols] = jnp.where(here, lane_value(msg, 1, o), 0.0)
            dep_x[rows, cols] = jnp.where(here, lane_value(msg, 2, o), 0.0)
    d = dep_x[...]
    mask = (d > 0.0).astype(f32)
    face = [jnp.minimum(d, beyond(d, a, b)) for a, b in ((0, 1), (0, -1), (1, 0), (-1, 0))]
    for i in range(4):
        faces[i] = face[i]
    diag = mask * (EPS + face[0] + face[1] + face[2] + face[3]) + (1.0 - mask)
    faces[4] = diag
    faces[5] = mask
    own = (ROWS, COLS)
    a_s = apply_faces(face + [diag], s_x[...])[own]
    sums = tile_sums([
        a_s * mask[own],
        mask[own],
        jnp.where(iota((R, L), 1) % 64 == 63, face[0][own], 0.0),
        jnp.where(iota((R, L), 0) % 4 == 3, face[2][own], 0.0),
        s * a_s,
        res[...] * s,
    ])
    pay[...] = jnp.broadcast_to(pack([q] + sums, lo % 8), (NDEV, H))


def step_kernel(got, coarse, w_in, q_in, res, s_x, faces, x0,
                r_out, s_out, as_out, x_out, d_out, ad_out, w_out, u_out, q_out, cu_out, net_out, num_out, pay):
    la, lo = lax.axis_index("lat"), lax.axis_index("lon")
    own = (ROWS, COLS)
    g = got[...]
    q, a, count, link_e, link_n, cc, ee = [unpack(g, f) for f in range(7)]
    w = w_in[...]
    tq = coarse_operator(q, count, link_e, link_n)
    u = a + tq
    d_a_d = total(cc + q * (2.0 * a + tq))
    rz = total(ee + w * q)
    alpha = rz / d_a_d
    w_out[...] = w - alpha * u
    u_out[...] = u
    net_out[0] = count
    net_out[1] = link_e
    net_out[2] = link_n
    num_out[0:1] = jnp.broadcast_to(rz, (1, H))
    num_out[1:2] = jnp.broadcast_to(d_a_d, (1, H))
    num_out[2:] = jnp.zeros((6, H), f32)
    cu = coarse_rows(coarse, u)
    q = q_in[0:1] - alpha * cu
    q_out[...] = jnp.broadcast_to(q, (8, H))
    cu_out[...] = jnp.broadcast_to(cu, (8, H))
    face = [faces[i] for i in range(6)]
    mask = face[5]
    s = s_x[...]
    d = s + mask * spread(got, la, lo)
    ad = apply_faces(face, d)
    s = s - alpha * (ad / face[4])
    a_s = apply_faces(face, s)[own]
    ad = ad[own]
    s = s[own]
    r = res[...] - alpha * ad
    r_out[...] = r
    s_out[...] = s
    as_out[...] = a_s
    x_out[...] = x0[...] + alpha * d[own]
    d_out[...] = d[own]
    ad_out[...] = ad
    sums = tile_sums([a_s * mask[own], s * a_s, r * s, s * ad])
    pay[...] = jnp.broadcast_to(pack([q] + sums, lo % 8), (NDEV, H))


def last_kernel(got, w_in, u_in, q1, cu0, net, num, coarse, res, scaled, a_s, ad, d_in, x_in, faces, surface, precond):
    la, lo = lax.axis_index("lat"), lax.axis_index("lon")
    own = (ROWS, COLS)
    g = got[...]
    q, a, cc, ee, hh = [unpack(g, f) for f in range(5)]
    w = w_in[...]
    u0 = u_in[...]
    rz0 = num[0:1, :1]
    dad0 = num[1:2, :1]
    tq = coarse_operator(q, net[0], net[1], net[2])
    zaz = total(cc + q * (2.0 * a + tq))
    rz = total(ee + w * q)
    zad = total(hh + q * u0)
    beta = rz / rz0
    alpha = rz / (zaz + 2.0 * beta * zad + beta * beta * dad0)
    p1, pu, pu0 = prolong_rows([q1[0:1], coarse_rows(coarse, a + tq), cu0[0:1]])
    q2 = p1 - alpha * (pu + beta * pu0)
    face = [faces[i] for i in range(6)]
    mask = face[5]
    pq = mask * spread(got, la, lo)
    d = scaled[...] + pq[own] + beta * d_in[...]
    ad1 = a_s[...] + apply_faces(face, pq)[own] + beta * ad[...]
    surface[...] = x_in[...] + alpha * d
    precond[...] = (res[...] - alpha * ad1) / face[4][own] + q2 * mask[own]


def swap_a(v, axis):
    return lax.ppermute(v, axis, [(i, i ^ 1) for i in range(16)])


def swap_b(v, axis):
    return lax.ppermute(v, axis, [(i, (i + 1 if i % 2 else i - 1) % 16) for i in range(16)])


def gather(pay):
    return lax.all_to_all(pay, BOTH, 0, 0, tiled=True)


def body(density, tend_east, tend_north, thickness, levels, ocean_mask, eta_prev, coarse):
    plane, wide = (R, L), (RX, LX)
    lon_msg, lat_msg = (R, LON_LANES), (LAT_ROWS, L)
    vm = pl.BlockSpec(memory_space=pltpu.VMEM)
    prefix, te, tn, wet, x0, depth, pe, pw, pn, ps, lat_a, lat_b, lon_a, lon_b = pl.pallas_call(
        levels_kernel,
        in_specs=[pl.BlockSpec(memory_space=pl.ANY)] * 7,
        out_specs=[vm] * 14,
        out_shape=[in_vmem(s) for s in [(2 * HALF, H)] + [plane] * 5 + ([lon_msg] * 2 + [lat_msg] * 2) + ([lat_msg] * 2 + [lon_msg] * 2)],
        scratch_shapes=[
            pltpu.SMEM((K,), f32),
            pltpu.VMEM(plane, jnp.int32),
            pltpu.VMEM(plane, jnp.int32),
            pltpu.VMEM(plane, f32),
            pltpu.VMEM((K, R, L), f32),
            pltpu.VMEM((K, R, L), f32),
            pltpu.VMEM((K, R, L), f32),
            pltpu.VMEM((2, R, L), f32),
            pltpu.SemaphoreType.DMA((3 * CHUNKS + 4,)),
        ],
        name="levels",
    )(thickness, levels, ocean_mask, eta_prev, density, tend_east, tend_north)
    lat_a, lat_b = swap_a(lat_a, "lat"), swap_b(lat_b, "lat")
    lon_a, lon_b = swap_a(lon_a, "lon"), swap_b(lon_b, "lon")
    fe, fn = call(
        inner_kernel,
        [plane, plane],
        "inner",
        scratch_shapes=[pltpu.VMEM((8, R, L), f32), pltpu.VMEM((8, R, L), f32)],
    )(prefix, wet, te, tn)
    r0, s0, dep_x, rows_a, rows_b, pay = call(
        residual_kernel,
        [plane, plane, wide, (8, L), (8, L), (NDEV, H)],
        "residual",
        scratch_shapes=[pltpu.VMEM(x, f32) for x in (lon_msg, lon_msg, lat_msg, lat_msg)],
    )(fe, fn, wet, x0, depth, pe, pw, pn, ps, lat_a, lat_b, lon_a, lon_b)
    rows_a, rows_b = swap_a(rows_a, "lat"), swap_b(rows_b, "lat")
    got = gather(pay)
    w0, q0, s_x, faces, pay = call(first_kernel, [G, (8, H), wide, (6,) + wide, (NDEV, H)], "first")(
        got, coarse, r0, s0, dep_x, rows_a, rows_b
    )
    got = gather(pay)
    r1, s1, as1, x1, d0, ad0, w1, u0, q1, cu0, net, num, pay = call(
        step_kernel, [plane] * 6 + [G, G, (8, H), (8, H), (3,) + G, (8, H), (NDEV, H)], "step"
    )(got, coarse, w0, q0, r0, s_x, faces, x0)
    got = gather(pay)
    return tuple(
        call(last_kernel, [plane, plane], "last", out=lambda s: jax.ShapeDtypeStruct(s, f32))(
            got, w1, u0, q1, cu0, net, num, coarse, r1, s1, as1, ad0, d0, x1, faces
        )
    )


def solution(mesh):
    return jax.shard_map(
        body,
        mesh=mesh,
        in_specs=(
            P(None, "lat", "lon"),
            P(None, "lat", "lon"),
            P(None, "lat", "lon"),
            P(),
            P("lat", "lon"),
            P("lat", "lon"),
            P("lat", "lon"),
            P(("lat", "lon"), None),
        ),
        out_specs=(P("lat", "lon"), P("lat", "lon")),
        check_vma=False,
    )
```

```python
import jax
import jax.numpy as jnp
from jax import lax
from jax.experimental import pallas as pl
from jax.experimental.pallas import tpu as pltpu
from jax.sharding import PartitionSpec as P

K = 75
R = 16
L = 256
H = 128
NLON = 16
NLAT = 16
NDEV = 256
EPS = 0.25
f32 = jnp.float32
highest = lax.Precision.HIGHEST
BOTH = ("lat", "lon")


def iota(shape, dim):
    return lax.broadcasted_iota(jnp.int32, shape, dim)


def in_vmem(shape):
    return pltpu.VMEM(shape, f32)


def call(kernel, out_shapes, name, out=in_vmem, **kw):
    vm = pl.BlockSpec(memory_space=pltpu.VMEM)

    def run(*args):
        return pl.pallas_call(
            kernel,
            out_shape=[out(s) for s in out_shapes],
            in_specs=[vm] * len(args),
            out_specs=[vm] * len(out_shapes),
            name=name,
            **kw,
        )(*[pltpu.with_memory_space_constraint(a, pltpu.VMEM) for a in args])

    return run


RX = R + 16
LX = L + 2 * H
ROWS = slice(8, 8 + R)
COLS = slice(H, H + L)


def beyond(v, rows, cols):
    n, m = v.shape
    if rows:
        v = pltpu.roll(v, -rows % n, 0)
    if cols:
        v = pltpu.roll(v, -cols % m, 1)
    return v


def apply_faces(faces, v):
    return faces[4] * v - (
        faces[0] * beyond(v, 0, 1)
        + faces[1] * beyond(v, 0, -1)
        + faces[2] * beyond(v, 1, 0)
        + faces[3] * beyond(v, -1, 0)
    )


def tile_sums(fields):
    n = len(fields)
    pick = (iota((L, H), 0) // 64 == iota((L, H), 1) % 4).astype(f32)
    cols = jnp.dot(jnp.concatenate(fields, axis=0), pick, precision=highest, preferred_element_type=f32)
    keep = iota((R, H), 0) // 4 == (iota((R, H), 1) % 16) // 4
    return [
        jnp.sum(jnp.where(keep, cols[R * i : R * i + R], 0.0), axis=0, keepdims=True)
        for i in range(n)
    ]


def pack(rows, rho):
    block = iota((1, H), 1) // 16
    out = jnp.zeros((1, H), f32)
    for f, row in enumerate(rows):
        out = jnp.where(block == (f + rho) % 8, row, out)
    return out


def unpack(got, f):
    shape = (NDEV // 8, 8, H)
    keep = iota(shape, 2) // 16 == (iota(shape, 1) + f) % 8
    flat = jnp.sum(jnp.where(keep, got.reshape(shape), 0.0), axis=1)
    return pltpu.roll(flat, (H - 16 * f) % H, 1) if f else flat


def coarse_rows(c_ref, w):
    acc = jnp.zeros((R, H), f32)
    for r in range(NDEV // 8):
        acc = acc + c_ref[:, H * r : H * r + H] * w[r : r + 1, :]
    col = jnp.sum(acc, axis=1, keepdims=True)
    return jnp.sum(jnp.where(iota((R, H), 0) == iota((R, H), 1) % 16, col, 0.0), axis=0, keepdims=True)


G = (NDEV // 8, H)


def c_east(q):
    lane = iota(G, 1)
    near = pltpu.roll(q, H - 1, 1)
    far = pltpu.roll(q, H - 13, 1)
    swap = jnp.where(iota(G, 0) % 2 == 0, pltpu.roll(far, G[0] - 1, 0), pltpu.roll(far, 1, 0))
    far = jnp.where(lane // 16 == 7, swap, far)
    return jnp.where(lane % 4 == 3, far, near)


def c_west(q):
    lane = iota(G, 1)
    near = pltpu.roll(q, 1, 1)
    far = pltpu.roll(q, 13, 1)
    swap = jnp.where(iota(G, 0) % 2 == 0, pltpu.roll(far, G[0] - 1, 0), pltpu.roll(far, 1, 0))
    far = jnp.where(lane // 16 == 0, swap, far)
    return jnp.where(lane % 4 == 0, far, near)


def c_north(q):
    near = pltpu.roll(q, H - 4, 1)
    far = pltpu.roll(pltpu.roll(q, 12, 1), G[0] - 2, 0)
    return jnp.where((iota(G, 1) % 16) // 4 == 3, far, near)


def c_south(q):
    near = pltpu.roll(q, 4, 1)
    far = pltpu.roll(pltpu.roll(q, H - 12, 1), 2, 0)
    return jnp.where((iota(G, 1) % 16) // 4 == 0, far, near)


def coarse_operator(q, count, link_e, link_n):
    flux_e = link_e * (q - c_east(q))
    flux_n = link_n * (q - c_north(q))
    return EPS * count * q + (flux_e - c_west(flux_e)) + (flux_n - c_south(flux_n))


def total(v):
    return jnp.sum(jnp.sum(v, axis=0, keepdims=True), axis=1, keepdims=True)


def neighbour(la, lo, da, do):
    a = la + da
    there = jnp.logical_and(a >= 0, a < NLAT)
    a = jnp.clip(a, 0, NLAT - 1)
    return a * NLON + (lo + do + NLON) % NLON, there


def lane_column(row, f, o):
    lane = iota((R, H), 1)
    hit = (lane // 16 == (f + o) % 8) & (lane % 16 == iota((R, H), 0))
    return jnp.sum(jnp.where(hit, jnp.broadcast_to(row, (R, H)), 0.0), axis=1, keepdims=True)


def lane_value(row, f, o):
    hit = iota((1, H), 1) == 16 * ((f + o) % 8)
    return jnp.sum(jnp.where(hit, row, 0.0), axis=1, keepdims=True)


def column_lanes(v, c):
    return jnp.sum(
        jnp.where(iota((R, H), 0) == iota((R, H), 1) % 16, v[:, c : c + 1], 0.0), axis=0, keepdims=True
    )


def spread(got_ref, la, lo):
    row = iota((RX, H), 0)
    lane = iota((RX, H), 1)
    ty = jnp.where(row < 8, 3, jnp.where(row < 8 + R, (row - 8) // 4, 0))
    src = jnp.zeros((RX, H), f32)
    l2 = iota((H, LX), 0)
    c2 = iota((H, LX), 1)
    pick = jnp.zeros((H, LX), f32)
    for do in (-1, 0, 1):
        o = (lo + do + NLON) % NLON
        south, mine, north = [
            jnp.broadcast_to(got_ref[pl.ds(neighbour(la, lo, da, do)[0], 1), :], (RX, H)) for da in (-1, 0, 1)
        ]
        part = jnp.where(row < 8, south, jnp.where(row < 8 + R, mine, north))
        src = jnp.where((lane // 16 == o % 8) & ((lane % 16) // 4 == ty), part, src)
        if do == 0:
            to = (c2 >= H) & (c2 < H + L) & (l2 % 4 == (c2 - H) // 64)
        elif do < 0:
            to = (c2 < H) & (l2 % 4 == 3)
        else:
            to = (c2 >= H + L) & (l2 % 4 == 0)
        pick = jnp.where(to & (l2 // 16 == o % 8), 1.0, pick)
    return jnp.dot(src, pick, precision=highest, preferred_element_type=f32)


def prolong_rows(rows):
    keep = (iota((R, H), 1) < 16) & (iota((R, H), 1) // 4 == iota((R, H), 0) // 4)
    pick = (iota((H, L), 0) % 4 == iota((H, L), 1) // 64).astype(f32)
    src = jnp.concatenate([jnp.where(keep, jnp.broadcast_to(q, (R, H)), 0.0) for q in rows], axis=0)
    out = jnp.dot(src, pick, precision=highest, preferred_element_type=f32)
    return [out[R * i : R * i + R] for i in range(len(rows))]


BOUNDS = (0, 30, 64, K)
CHUNKS = len(BOUNDS) - 1
NEAR = 0
FAR = 80
M_FORCE, M_WET1, M_WET2, M_DEPTH1, M_DEPTH2, M_X = range(6)
LAT_MISC = 160
HALF = FAR * R
LAT_ROWS = 168
LON_MISC = 3 * K
LON_LANES = 2 * H
C1, C2 = 8.0 / 12.0, 1.0 / 12.0


def lon_pick(prof, m, col):
    at = 3 * m.astype(jnp.int32) - 3 + col
    lane = iota(prof.shape, 1)
    return jnp.sum(jnp.where((lane == at) & (m > 0.0), prof, 0.0), axis=1, keepdims=True)


def lat_pick(prof, m):
    level = iota((FAR, L), 0).astype(f32) + 1.0
    return jnp.sum(jnp.where(level == m, prof, 0.0), axis=0, keepdims=True)


def levels_kernel(thick, levels, mask, eta, rho, te, tn,
                  prefix, fe_out, fn_out, wet_out, x_out, depth_out, pe, pw, pn, ps, lat_a, lat_b, lon_a, lon_b,
                  t_s, lev_v, mask_v, eta_v, rho_v, te_v, tn_v, run, sem):
    small = [
        pltpu.make_async_copy(a, b, sem.at[3 * CHUNKS + i])
        for i, (a, b) in enumerate(((thick, t_s), (levels, lev_v), (mask, mask_v), (eta, eta_v)))
    ]
    for c in small:
        c.start()
    big = [[], [], []]
    arrays = ((rho, rho_v), (te, te_v), (tn, tn_v))
    for i, c in [(0, c) for c in range(CHUNKS)] + [(i, c) for c in range(CHUNKS) for i in (1, 2)]:
        part = pl.ds(BOUNDS[c], BOUNDS[c + 1] - BOUNDS[c])
        a, b = arrays[i]
        big[i].append(pltpu.make_async_copy(a.at[part], b.at[part], sem.at[CHUNKS * i + c]))
        big[i][-1].start()
    for c in small:
        c.wait()
    own = (lev_v[...] * mask_v[...]).astype(f32)
    wet_out[...] = own
    x_out[...] = mask_v[...].astype(f32) * eta_v[...]
    zero = jnp.zeros((8, H), f32)
    lane8 = iota((8, H), 1)
    blocks = [(a, b, slice(8 * a, 8 * a + 8), slice(H * b, H * b + H)) for a in range(2) for b in range(2)]
    for c in range(CHUNKS):
        big[0][c].wait()
        state = []
        for a, b, rs, ls in blocks:
            lon_out = pe if b else pw
            if c == 0:
                state.append([zero] * 4)
            else:
                state.append([run[0, rs, ls], run[1, rs, ls], lon_out[rs, :H], lon_out[rs, H:]])
        for k in range(BOUNDS[c], BOUNDS[c + 1]):
            t = t_s[k]
            at = 3 * k
            halves = [(h, (lane8 >= at - H * h) & (lane8 < at - H * h + 3)) for h in (0, 1) if at < H * h + H and at + 2 >= H * h]
            for (a, b, rs, ls), v in zip(blocks, state):
                v[0] = v[0] + t * rho_v[k, rs, ls]
                v[1] = g = v[1] + t * v[0]
                prefix[HALF * b + R * k + 8 * a : HALF * b + R * k + 8 * a + 8, :] = g
                shift = (at + 3 * b) % H
                moved = pltpu.roll(g, shift, 1) if shift else g
                for h, here in halves:
                    v[2 + h] = jnp.where(here, moved, v[2 + h])
        for (a, b, rs, ls), v in zip(blocks, state):
            lon_out = pe if b else pw
            run[0, rs, ls], run[1, rs, ls] = v[0], v[1]
            lon_out[rs, :H] = v[2]
            lon_out[rs, H:] = v[3]
    x = x_out[...]
    lane_t = iota((R, H), 1)

    def column(v, c):
        return v[:, c : c + 1]

    def line(v, r):
        return v[r : r + 1]

    def profile(r):
        return jnp.concatenate([prefix[pl.ds(HALF * b + r, FAR, stride=R), :] for b in range(2)], axis=1)

    added = []
    for out, past_at, c0, c1, c2 in ((pe, 0, L - 1, L - 2, L - 3), (pw, 2, 0, 1, 2)):
        o = column(own, c0)
        near = lon_pick(out[...], jnp.minimum(o, column(own, c1)), 1)
        past = lon_pick(out[...], jnp.minimum(o, column(own, c2)), past_at)
        added.append(C1 * near - C2 * past)
        tile = out[:, H:]
        for i, v in ((M_WET1, o), (M_WET2, column(own, c1)), (M_X, column(x, c0))):
            tile = jnp.where(lane_t == LON_MISC - H + i, v, tile)
        out[:, H:] = tile
    for out, r0, r1, r2 in ((pn, R - 1, R - 2, R - 3), (ps, 0, 1, 2)):
        out[NEAR : NEAR + FAR] = profile(r0)
        far = profile(r1)
        out[FAR : 2 * FAR] = far
        o = line(own, r0)
        near = lat_pick(far, jnp.minimum(o, line(own, r1)))
        past = lat_pick(profile(r2), jnp.minimum(o, line(own, r2)))
        added.append(C1 * near - C2 * past)
        for i, v in ((M_WET1, o), (M_WET2, line(own, r1)), (M_X, line(x, r0))):
            out[LAT_MISC + i : LAT_MISC + i + 1] = v
    lat_even = lax.axis_index("lat") % 2 == 0
    n, s = pn[...], ps[...]
    lat_a[...] = jnp.where(lat_even, n, s)
    lat_b[...] = jnp.where(lat_even, s, n)
    for c in range(CHUNKS):
        big[1][c].wait()
        big[2][c].wait()
        for a, b, rs, ls in blocks:
            d, fe, fn = [v[rs, ls] if c else zero for v in (depth_out, fe_out, fn_out)]
            wet = wet_out[rs, ls]
            for k in range(BOUNDS[c], BOUNDS[c + 1]):
                ta = jnp.where(wet > float(k), t_s[k], 0.0)
                d = d + ta
                fe = fe + ta * te_v[k, rs, ls]
                fn = fn + ta * tn_v[k, rs, ls]
            depth_out[rs, ls] = d
            fe_out[rs, ls] = fe
            fn_out[rs, ls] = fn
    d, fe, fn = depth_out[...], fe_out[...], fn_out[...]
    for out, add, c0, c1 in ((pe, added[0], L - 1, L - 2), (pw, -added[1], 0, 1)):
        tile = out[:, H:]
        for i, v in ((M_FORCE, column(fe, c0) + add), (M_DEPTH1, column(d, c0)), (M_DEPTH2, column(d, c1))):
            tile = jnp.where(lane_t == LON_MISC - H + i, v, tile)
        out[:, H:] = tile
    lon_even = lax.axis_index("lon") % 2 == 0
    e, w = pe[...], pw[...]
    lon_a[...] = jnp.where(lon_even, e, w)
    lon_b[...] = jnp.where(lon_even, w, e)
    for i, n, s in (
        (M_FORCE, line(fn, R - 1) + added[2], line(fn, 0) - added[3]),
        (M_DEPTH1, line(d, R - 1), line(d, 0)),
        (M_DEPTH2, line(d, R - 2), line(d, 1)),
    ):
        lat_a[LAT_MISC + i : LAT_MISC + i + 1] = jnp.where(lat_even, n, s)
        lat_b[LAT_MISC + i : LAT_MISC + i + 1] = jnp.where(lat_even, s, n)


def inner_kernel(prefix, wet, te, tn, fe_out, fn_out, m8, a8):
    own = wet[...]
    lane = iota((R, L), 1)
    row = iota((R, L), 0)
    for d, n in enumerate((1, 2)):
        m8[d] = jnp.where(lane < L - n, jnp.minimum(own, beyond(own, 0, n)), 0.0)
        m8[2 + d] = jnp.where(lane >= n, jnp.minimum(own, beyond(own, 0, -n)), 0.0)
        m8[4 + d] = jnp.where(row < R - n, jnp.minimum(own, beyond(own, n, 0)), 0.0)
        m8[6 + d] = jnp.where(row >= n, jnp.minimum(own, beyond(own, -n, 0)), 0.0)
    for a in range(2):
        for b in range(2):
            rs, ls = slice(8 * a, 8 * a + 8), slice(H * b, H * b + H)
            m = [m8[i, rs, ls] for i in range(8)]
            acc = [jnp.zeros((8, H), f32)] * 8
            for k in range(K):
                g = prefix[HALF * b + R * k + 8 * a : HALF * b + R * k + 8 * a + 8, :]
                acc = [jnp.where(mi > float(k), g, ai) for mi, ai in zip(m, acc)]
            for i in range(8):
                a8[i, rs, ls] = acc[i]
    fe_out[...] = te[...] + C1 * (beyond(a8[0], 0, -1) - beyond(a8[2], 0, 1)) - C2 * (
        beyond(a8[1], 0, -2) - beyond(a8[3], 0, 2)
    )
    fn_out[...] = tn[...] + C1 * (beyond(a8[4], -1, 0) - beyond(a8[6], 1, 0)) - C2 * (
        beyond(a8[5], -2, 0) - beyond(a8[7], 2, 0)
    )


def residual_kernel(fe_in, fn_in, wet, x0, depth, pe, pw, pn, ps, lat_a, lat_b, lon_a, lon_b,
                    res, scaled, dep_x, rows_a, rows_b, pay):
    own = wet[...]
    la, lo = lax.axis_index("lat"), lax.axis_index("lon")
    lat_even, lon_even = la % 2 == 0, lo % 2 == 0
    a, b = lat_a[...], lat_b[...]
    gn = jnp.where(lat_even, a, b)
    gs = jnp.where(lat_even, b, a)
    a, b = lon_a[...], lon_b[...]
    ge = jnp.where(lon_even, a, b)
    gw = jnp.where(lon_even, b, a)
    lane = iota((R, L), 1)
    row = iota((R, L), 0)

    def lon_misc(ref, i):
        return ref[:, LON_MISC + i : LON_MISC + i + 1]

    def lat_misc(ref, i):
        there = la < NLAT - 1 if ref is gn else la > 0
        return jnp.where(there, ref[LAT_MISC + i : LAT_MISC + i + 1], 0.0)

    def from_lon(ref, m, col):
        return lon_pick(ref[...], m, col)

    def from_lat(ref, m, col):
        return lat_pick(ref[FAR : 2 * FAR] if col else ref[NEAR : NEAR + FAR], m)

    def cross(pick, got, sent, o1, o2, n1, n2, got_near, sent_near):
        gn_, sn_ = (got_near, 1), (sent_near, 1)
        first = (-8.0 * pick(got, jnp.minimum(o1, n1), gn_[0]) + pick(got, jnp.minimum(o1, n2), gn_[1])) / 12.0
        second = pick(got, jnp.minimum(o2, n1), gn_[0]) / 12.0
        theirs = (8.0 * pick(sent, jnp.minimum(n1, o1), sn_[0]) - pick(sent, jnp.minimum(n1, o2), sn_[1])) / 12.0
        return first, second, theirs

    fe = fe_in[...]
    fn = fn_in[...]
    a, b, far_e = cross(from_lon, ge, pe, own[:, L - 1 :], own[:, L - 2 : L - 1],
                        lon_misc(ge, M_WET1), lon_misc(ge, M_WET2), 0, 2)
    fe = fe + jnp.where(lane == L - 1, a, 0.0) + jnp.where(lane == L - 2, b, 0.0)
    fe_e = lon_misc(ge, M_FORCE) + far_e
    a, b, far_w = cross(from_lon, gw, pw, own[:, :1], own[:, 1:2],
                        lon_misc(gw, M_WET1), lon_misc(gw, M_WET2), 2, 0)
    fe = fe - jnp.where(lane == 0, a, 0.0) - jnp.where(lane == 1, b, 0.0)
    fe_w = lon_misc(gw, M_FORCE) - far_w
    a, b, far_n = cross(from_lat, gn, pn, own[R - 1 :], own[R - 2 : R - 1],
                        lat_misc(gn, M_WET1), lat_misc(gn, M_WET2), 0, 0)
    fn = fn + jnp.where(row == R - 1, a, 0.0) + jnp.where(row == R - 2, b, 0.0)
    fn_n = lat_misc(gn, M_FORCE) + far_n
    a, b, far_s = cross(from_lat, gs, ps, own[:1], own[1:2],
                        lat_misc(gs, M_WET1), lat_misc(gs, M_WET2), 0, 0)
    fn = fn - jnp.where(row == 0, a, 0.0) - jnp.where(row == 1, b, 0.0)
    fn_s = lat_misc(gs, M_FORCE) - far_s

    def shifts(v, e, w, n, s):
        return (
            jnp.where(lane == L - 1, e, beyond(v, 0, 1)),
            jnp.where(lane == 0, w, beyond(v, 0, -1)),
            jnp.where(row == R - 1, n, beyond(v, 1, 0)),
            jnp.where(row == 0, s, beyond(v, -1, 0)),
        )

    mask = (own > 0.0).astype(f32)
    d = depth[...]
    x = x0[...]
    face = [
        jnp.minimum(d, v)
        for v in shifts(d, lon_misc(ge, M_DEPTH1), lon_misc(gw, M_DEPTH1), lat_misc(gn, M_DEPTH1), lat_misc(gs, M_DEPTH1))
    ]
    diag = mask * (EPS + face[0] + face[1] + face[2] + face[3]) + (1.0 - mask)
    ax = diag * x
    for f, v in zip(face, shifts(x, lon_misc(ge, M_X), lon_misc(gw, M_X), lat_misc(gn, M_X), lat_misc(gs, M_X))):
        ax = ax - f * v
    f_e, f_w, _, _ = shifts(fe, fe_e, fe_w, fn_n, fn_s)
    _, _, f_n, f_s = shifts(fn, fe_e, fe_w, fn_n, fn_s)
    r = mask * 0.5 * (f_w - f_e + f_s - f_n) - ax
    s = r / diag
    res[...] = r
    scaled[...] = s
    rows_a[...] = jnp.where(lat_even, s[8:], s[:8])
    rows_b[...] = jnp.where(lat_even, s[:8], s[8:])
    dep_x[...] = jnp.zeros((RX, LX), f32)
    dep_x[ROWS, COLS] = d
    dep_x[7:8, COLS] = lat_misc(gs, M_DEPTH1)
    dep_x[6:7, COLS] = lat_misc(gs, M_DEPTH2)
    dep_x[8 + R : 9 + R, COLS] = lat_misc(gn, M_DEPTH1)
    dep_x[9 + R : 10 + R, COLS] = lat_misc(gn, M_DEPTH2)
    lane_t = iota((R, H), 1)
    dep_x[ROWS, :H] = jnp.where(
        lane_t == H - 1, lon_misc(gw, M_DEPTH1), jnp.where(lane_t == H - 2, lon_misc(gw, M_DEPTH2), 0.0)
    )
    dep_x[ROWS, H + L :] = jnp.where(
        lane_t == 0, lon_misc(ge, M_DEPTH1), jnp.where(lane_t == 1, lon_misc(ge, M_DEPTH2), 0.0)
    )
    rho = lo % 8
    (w,) = tile_sums([r * mask])
    pay[...] = jnp.broadcast_to(pack([w], rho), (NDEV, H))
    for do, c1, c2 in ((1, L - 1, L - 2), (-1, 0, 1)):
        at, _ = neighbour(la, lo, 0, do)
        pay[pl.ds(at, 1), :] = pack([w, column_lanes(s, c1), column_lanes(s, c2)], rho)
        for da, j in ((1, R - 1), (-1, 0)):
            at, there = neighbour(la, lo, da, do)
            at = jnp.where(there, at, la * NLON + lo)
            pay[pl.ds(at, 1), :] = pack(
                [w, jnp.broadcast_to(s[j : j + 1, c1 : c1 + 1], (1, H)), jnp.broadcast_to(d[j : j + 1, c1 : c1 + 1], (1, H))],
                rho,
            )


def first_kernel(got, coarse, res, scaled, dep_in, rows_a, rows_b, w_out, q_out, s_x, faces, pay):
    la, lo = lax.axis_index("lat"), lax.axis_index("lon")
    even = la % 2 == 0
    a, b = rows_a[...], rows_b[...]
    sn, ss = jnp.where(even, a, b), jnp.where(even, b, a)
    w = unpack(got[...], 0)
    w_out[...] = w
    q = coarse_rows(coarse, w)
    q_out[...] = jnp.broadcast_to(q, (8, H))
    s = scaled[...]
    s_x[ROWS, COLS] = s
    s_x[:8, COLS] = jnp.where(la > 0, ss, 0.0)
    s_x[8 + R :, COLS] = jnp.where(la < NLAT - 1, sn, 0.0)
    lane = iota((R, H), 1)
    dep = dep_in[...]
    dep_x = faces.at[4]
    dep_x[...] = dep
    for do, cols, l1, l2 in ((1, slice(H + L, LX), 0, 1), (-1, slice(0, H), H - 1, H - 2)):
        at, _ = neighbour(la, lo, 0, do)
        o = (lo + do + NLON) % NLON
        msg = got[pl.ds(at, 1), :]
        s_x[ROWS, cols] = jnp.where(lane == l1, lane_column(msg, 1, o), jnp.where(lane == l2, lane_column(msg, 2, o), 0.0))
        for da, rows, j in ((1, slice(8 + R, RX), 0), (-1, slice(0, 8), 7)):
            at, there = neighbour(la, lo, da, do)
            msg = got[pl.ds(at, 1), :]
            here = (iota((8, H), 0) == j) & (iota((8, H), 1) == l1) & there
            s_x[rows, cols] = jnp.where(here, lane_value(msg, 1, o), 0.0)
            dep_x[rows, cols] = jnp.where(here, lane_value(msg, 2, o), 0.0)
    d = dep_x[...]
    mask = (d > 0.0).astype(f32)
    face = [jnp.minimum(d, beyond(d, a, b)) for a, b in ((0, 1), (0, -1), (1, 0), (-1, 0))]
    for i in range(4):
        faces[i] = face[i]
    diag = mask * (EPS + face[0] + face[1] + face[2] + face[3]) + (1.0 - mask)
    faces[4] = diag
    faces[5] = mask
    own = (ROWS, COLS)
    a_s = apply_faces(face + [diag], s_x[...])[own]
    sums = tile_sums([
        a_s * mask[own],
        mask[own],
        jnp.where(iota((R, L), 1) % 64 == 63, face[0][own], 0.0),
        jnp.where(iota((R, L), 0) % 4 == 3, face[2][own], 0.0),
        s * a_s,
        res[...] * s,
    ])
    pay[...] = jnp.broadcast_to(pack([q] + sums, lo % 8), (NDEV, H))


def step_kernel(got, coarse, w_in, q_in, res, s_x, faces, x0,
                r_out, s_out, as_out, x_out, d_out, ad_out, w_out, u_out, q_out, cu_out, net_out, num_out, pay):
    la, lo = lax.axis_index("lat"), lax.axis_index("lon")
    own = (ROWS, COLS)
    g = got[...]
    q, a, count, link_e, link_n, cc, ee = [unpack(g, f) for f in range(7)]
    w = w_in[...]
    tq = coarse_operator(q, count, link_e, link_n)
    u = a + tq
    d_a_d = total(cc + q * (2.0 * a + tq))
    rz = total(ee + w * q)
    alpha = rz / d_a_d
    w_out[...] = w - alpha * u
    u_out[...] = u
    net_out[0] = count
    net_out[1] = link_e
    net_out[2] = link_n
    num_out[0:1] = jnp.broadcast_to(rz, (1, H))
    num_out[1:2] = jnp.broadcast_to(d_a_d, (1, H))
    num_out[2:] = jnp.zeros((6, H), f32)
    cu = coarse_rows(coarse, u)
    q = q_in[0:1] - alpha * cu
    q_out[...] = jnp.broadcast_to(q, (8, H))
    cu_out[...] = jnp.broadcast_to(cu, (8, H))
    face = [faces[i] for i in range(6)]
    mask = face[5]
    s = s_x[...]
    d = s + mask * spread(got, la, lo)
    ad = apply_faces(face, d)
    s = s - alpha * (ad / face[4])
    a_s = apply_faces(face, s)[own]
    ad = ad[own]
    s = s[own]
    r = res[...] - alpha * ad
    r_out[...] = r
    s_out[...] = s
    as_out[...] = a_s
    x_out[...] = x0[...] + alpha * d[own]
    d_out[...] = d[own]
    ad_out[...] = ad
    sums = tile_sums([a_s * mask[own], s * a_s, r * s, s * ad])
    pay[...] = jnp.broadcast_to(pack([q] + sums, lo % 8), (NDEV, H))


def last_kernel(got, w_in, u_in, q1, cu0, net, num, coarse, res, scaled, a_s, ad, d_in, x_in, faces, surface, precond):
    la, lo = lax.axis_index("lat"), lax.axis_index("lon")
    own = (ROWS, COLS)
    g = got[...]
    q, a, cc, ee, hh = [unpack(g, f) for f in range(5)]
    w = w_in[...]
    u0 = u_in[...]
    rz0 = num[0:1, :1]
    dad0 = num[1:2, :1]
    tq = coarse_operator(q, net[0], net[1], net[2])
    zaz = total(cc + q * (2.0 * a + tq))
    rz = total(ee + w * q)
    zad = total(hh + q * u0)
    beta = rz / rz0
    alpha = rz / (zaz + 2.0 * beta * zad + beta * beta * dad0)
    p1, pu, pu0 = prolong_rows([q1[0:1], coarse_rows(coarse, a + tq), cu0[0:1]])
    q2 = p1 - alpha * (pu + beta * pu0)
    face = [faces[i] for i in range(6)]
    mask = face[5]
    pq = mask * spread(got, la, lo)
    d = scaled[...] + pq[own] + beta * d_in[...]
    ad1 = a_s[...] + apply_faces(face, pq)[own] + beta * ad[...]
    surface[...] = x_in[...] + alpha * d
    precond[...] = (res[...] - alpha * ad1) / face[4][own] + q2 * mask[own]


def swap_a(v, axis):
    return lax.ppermute(v, axis, [(i, i ^ 1) for i in range(16)])


def swap_b(v, axis):
    return lax.ppermute(v, axis, [(i, (i + 1 if i % 2 else i - 1) % 16) for i in range(16)])


def gather(pay):
    return lax.all_to_all(pay, BOTH, 0, 0, tiled=True)


def body(density, tend_east, tend_north, thickness, levels, ocean_mask, eta_prev, coarse):
    plane, wide = (R, L), (RX, LX)
    lon_msg, lat_msg = (R, LON_LANES), (LAT_ROWS, L)
    vm = pl.BlockSpec(memory_space=pltpu.VMEM)
    prefix, te, tn, wet, x0, depth, pe, pw, pn, ps, lat_a, lat_b, lon_a, lon_b = pl.pallas_call(
        levels_kernel,
        in_specs=[pl.BlockSpec(memory_space=pl.ANY)] * 7,
        out_specs=[vm] * 14,
        out_shape=[in_vmem(s) for s in [(2 * HALF, H)] + [plane] * 5 + ([lon_msg] * 2 + [lat_msg] * 2) + ([lat_msg] * 2 + [lon_msg] * 2)],
        scratch_shapes=[
            pltpu.SMEM((K,), f32),
            pltpu.VMEM(plane, jnp.int32),
            pltpu.VMEM(plane, jnp.int32),
            pltpu.VMEM(plane, f32),
            pltpu.VMEM((K, R, L), f32),
            pltpu.VMEM((K, R, L), f32),
            pltpu.VMEM((K, R, L), f32),
            pltpu.VMEM((2, R, L), f32),
            pltpu.SemaphoreType.DMA((3 * CHUNKS + 4,)),
        ],
        name="levels",
    )(thickness, levels, ocean_mask, eta_prev, density, tend_east, tend_north)
    lat_a, lat_b = swap_a(lat_a, "lat"), swap_b(lat_b, "lat")
    lon_a, lon_b = swap_a(lon_a, "lon"), swap_b(lon_b, "lon")
    fe, fn = call(
        inner_kernel,
        [plane, plane],
        "inner",
        scratch_shapes=[pltpu.VMEM((8, R, L), f32), pltpu.VMEM((8, R, L), f32)],
    )(prefix, wet, te, tn)
    r0, s0, dep_x, rows_a, rows_b, pay = call(
        residual_kernel,
        [plane, plane, wide, (8, L), (8, L), (NDEV, H)],
        "residual",
    )(fe, fn, wet, x0, depth, pe, pw, pn, ps, lat_a, lat_b, lon_a, lon_b)
    rows_a, rows_b = swap_a(rows_a, "lat"), swap_b(rows_b, "lat")
    got = gather(pay)
    w0, q0, s_x, faces, pay = call(first_kernel, [G, (8, H), wide, (6,) + wide, (NDEV, H)], "first")(
        got, coarse, r0, s0, dep_x, rows_a, rows_b
    )
    got = gather(pay)
    r1, s1, as1, x1, d0, ad0, w1, u0, q1, cu0, net, num, pay = call(
        step_kernel, [plane] * 6 + [G, G, (8, H), (8, H), (3,) + G, (8, H), (NDEV, H)], "step"
    )(got, coarse, w0, q0, r0, s_x, faces, x0)
    got = gather(pay)
    return tuple(
        call(last_kernel, [plane, plane], "last", out=lambda s: jax.ShapeDtypeStruct(s, f32))(
            got, w1, u0, q1, cu0, net, num, coarse, r1, s1, as1, ad0, d0, x1, faces
        )
    )


def solution(mesh):
    return jax.shard_map(
        body,
        mesh=mesh,
        in_specs=(
            P(None, "lat", "lon"),
            P(None, "lat", "lon"),
            P(None, "lat", "lon"),
            P(),
            P("lat", "lon"),
            P("lat", "lon"),
            P("lat", "lon"),
            P(("lat", "lon"), None),
        ),
        out_specs=(P("lat", "lon"), P("lat", "lon")),
        check_vma=False,
    )
```
